32 devices in a mesh: rep: 4 (over x, core), space: 8 (over z, y).
Axes of the slice: x: 2, y: 2, z: 4, core: 2. Of those that a mesh axis runs over, the one named last changes fastest.
Arguments:
- phase_space: float32 [4, 6, 4, 16384], P('rep', None, None, 'space'), may hold values from -6 to 6
- charges: float32 [4, 4, 16384], P('rep', None, 'space'), may hold values from -4 to 4
- lj_depth: float32 [4, 4, 16384], P('rep', None, 'space'), may hold values from 0.5 to 2
- cluster_fill: int32 [4, 16384], P('rep', 'space'), may hold values from 1 to 4
- neighbours: int32 [4, 16, 16384], P('rep', None, 'space'), may hold values from 0 to 3071
- ghost_send: int32 [4, 8192], P('rep', 'space'), may hold values from 0 to 2047
- partner: int32 [4], replicated, may hold values from 0 to 3, as said below
- scale_order: int32 [4], replicated, may hold values from 0 to 3, as said below
- coupling: float32 [4], replicated, may hold values from 0.25 to 1
Outputs:
- advanced: float32 [4, 6, 4, 16384], P('rep', None, None, 'space')
The draws below stay inside these ranges and needn't reach their ends.
Inputs may be any that keep to these rules, and one draw needn't show every extreme that they name: partner[l] is l - 1, l or l + 1, and partner[partner[l]] = l; for one p of 0 or 1, the same for the whole matching, every swapped pair is (2k + p, 2k + p + 1). `scale_order`: each level once.
All inputs are finite; a program needn't handle non-finite values.
Results may differ from the reference program's by a relative error of at most 0.0003.
Values sent between devices are 32-bit elements; how exact they have to be, the bound alone decides.
A program may use at most 128 MiB of HBM per device.

```python
import math
import jax
import jax.numpy as jnp
from jax import lax

CS = 4
NB = 16
STEPS = 2
NCL = 2048
LEVELS = 4
GHOST = 512
NCLT = 16384
N_SPACE = 8


def draw_partner(key, part):
    phase_bit = jax.random.randint(jax.random.fold_in(key, 11), (), 0, 2)
    accepted = jax.random.randint(jax.random.fold_in(key, 12), (LEVELS,), 0, 2)
    levels = jnp.arange(LEVELS, dtype=jnp.int32)
    pair_low = levels - (levels - phase_bit) % 2
    usable = (pair_low >= 0) & (pair_low + 1 < LEVELS)
    taken = (accepted[jnp.clip(pair_low, 0, LEVELS - 1)] == 1) & usable
    moved = jnp.where(levels == pair_low, levels + 1, levels - 1)
    return jnp.where(taken, moved, levels).astype(jnp.int32)


def draw_scale_order(key, part):
    order = jax.random.permutation(jax.random.fold_in(key, 21), LEVELS).astype(jnp.int32)
    target = jax.random.randint(jax.random.fold_in(key, 22), (), 2, LEVELS).astype(jnp.int32)
    levels = jnp.arange(LEVELS, dtype=jnp.int32)
    holder = jnp.sum(jnp.where(order == target, levels, 0)).astype(jnp.int32)
    first = order[0]
    result = jnp.where(levels == 0, target, jnp.where(levels == holder, first, order))
    return result.astype(jnp.int32)


def touch_ends(values, own_key, least, largest):
    longest = values.shape.index(max(values.shape))
    spots = []
    for shift in (0, 1):
        where = [jax.random.randint(jax.random.fold_in(own_key, axis), (), 0, length) for axis, length in enumerate(values.shape)]
        where[longest] = (where[longest] + shift) % values.shape[longest]
        spots.append(tuple(where))
    return values.at[spots[0]].set(least).at[spots[1]].set(largest)


def level_of(key, extent, shards, low, top_value):
    factor_of, own = 1.0, jax.random.fold_in(key, 6)
    for axis_at, blocks in shards:
        draws = jnp.exp(jax.random.uniform(jax.random.fold_in(own, axis_at), (blocks,), jnp.float32, low / len(shards), top_value / len(shards)))
        factor_of = factor_of * jnp.repeat(draws, extent[axis_at] // blocks).reshape([-1 if axis == axis_at else 1 for axis in range(len(extent))])
    return factor_of


def scatter_about(rng, shape, scale, bound, pieces=(), kind=jnp.bfloat16):
    gain = level_of(rng, shape, pieces, -0.22, 0.18) if pieces else 1.0
    array = jax.random.normal(rng, shape, jnp.float32) * scale * gain
    return jnp.minimum(jnp.maximum(array, -bound), bound).astype(kind)


def setup_inputs(seed: int = 0) -> dict:
    streams_of = jax.random.split(jax.random.key(seed), 10)
    return {
        "phase_space": scatter_about(streams_of[0], (LEVELS, 6, CS, NCLT), 1.0, 6.0, ((0, 4), (3, 8)), jnp.float32),
        "charges": scatter_about(streams_of[1], (LEVELS, CS, NCLT), 1.0, 4.0, ((0, 4), (2, 8)), jnp.float32),
        "lj_depth": jnp.clip(jnp.exp(math.log(2.0) - 1.3862944 * jax.random.uniform(streams_of[2], (LEVELS, CS, NCLT), jnp.float32) ** level_of(streams_of[2], (LEVELS, CS, NCLT), ((0, 4), (2, 8)), -0.2, 0.2)), 0.5, 2.0),
        "cluster_fill": touch_ends(jax.random.randint(streams_of[3], (LEVELS, NCLT), 1, 5), jax.random.fold_in(streams_of[3], 1), 1, 4).astype(jnp.int32),
        "neighbours": touch_ends(jax.random.randint(streams_of[4], (LEVELS, NB, NCLT), 0, NCL + 2 * GHOST), jax.random.fold_in(streams_of[4], 1), 0, (NCL + 2 * GHOST) - 1).astype(jnp.int32),
        "ghost_send": touch_ends(jax.random.randint(streams_of[5], (LEVELS, 2 * GHOST * N_SPACE), 0, NCL), jax.random.fold_in(streams_of[5], 1), 0, NCL - 1).astype(jnp.int32),
        "partner": draw_partner(jax.random.fold_in(streams_of[9], 71), 0),
        "scale_order": draw_scale_order(jax.random.fold_in(streams_of[9], 71), 0),
        "coupling": jnp.clip(jnp.exp(jax.random.uniform(streams_of[8], (LEVELS,), jnp.float32, math.log(0.25), math.log(1.0))), 0.25, 1.0),
    }


time_step = 0.2
softening = 0.5

def cluster_forces(positions, params, pool_pos, pool_par, near_list, strength):
    total = positions.shape[2]
    block_size = min(512, total)
    block_count = total // block_size

    def block_forces(block_id):
        first_row = (block_id * block_size).astype(jnp.int32)
        own_pos = lax.dynamic_slice_in_dim(positions, first_row, block_size, 2)
        own_par = lax.dynamic_slice_in_dim(params, first_row, block_size, 2)
        slot_ids = lax.dynamic_slice_in_dim(near_list, first_row, block_size, 1)
        other_pos = pool_pos[:, :, slot_ids]
        other_par = pool_par[:, :, slot_ids]
        offset = own_pos[:, :, None, None, :] - other_pos[:, None]
        inverse = 1.0 / (lax.optimization_barrier(jnp.sum(offset * offset, axis=0)) + softening)
        charge_pair = own_par[0][:, None, None, :] * other_par[0][None]
        depth_pair = own_par[1][:, None, None, :] * other_par[1][None]
        weight = strength * charge_pair * inverse * jnp.sqrt(inverse) + depth_pair * (inverse ** 3 - inverse ** 2)
        return lax.optimization_barrier(jnp.sum(weight[None] * offset, axis=(2, 3)))
    stacked = lax.map(block_forces, jnp.arange(block_count, dtype=jnp.int32))
    return jnp.moveaxis(stacked, 0, 2).reshape(3, positions.shape[1], total)

def reference(phase_space, charges, lj_depth, cluster_fill, neighbours, ghost_send, partner, scale_order, coupling):
    swapped = phase_space[partner]
    couplings = coupling[scale_order]
    send_lists = ghost_send.reshape(LEVELS, N_SPACE, 2 * GHOST)

    def run_level(level_data):
        phase_now, charge_row, depth_row, fill_row, near_level, sender_level, strength = level_data
        atom_slot = jnp.arange(CS, dtype=jnp.int32)[:, None]
        present = (atom_slot < fill_row[None, :]).astype(jnp.float32)
        params = jnp.stack([charge_row * present, depth_row * present]).reshape(2, CS, N_SPACE, NCL)
        phase_now = phase_now.reshape(6, CS, N_SPACE, NCL)
        positions = phase_now[:3]
        velocity = phase_now[3:]
        near_level = near_level.reshape(NB, N_SPACE, NCL)
        for step_index in range(STEPS):
            packet = jnp.concatenate([positions, params], 0)

            def device_forces(device):
                lower = (device - 1) % N_SPACE
                upper = (device + 1) % N_SPACE
                from_lower = jnp.take(packet[:, :, lower], sender_level[lower][GHOST:], axis=2)
                from_upper = jnp.take(packet[:, :, upper], sender_level[upper][:GHOST], axis=2)
                pool = jnp.concatenate([packet[:, :, device], from_lower, from_upper], 2)
                return cluster_forces(positions[:, :, device], params[:, :, device], pool[:3], pool[3:], near_level[:, device], strength)
            forces = lax.map(device_forces, jnp.arange(N_SPACE, dtype=jnp.int32))
            forces = jnp.moveaxis(forces, 0, 2)
            velocity = velocity + time_step * forces
            positions = positions + time_step * velocity
        return jnp.concatenate([positions, velocity], 0).reshape(6, CS, N_SPACE * NCL)
    return lax.map(run_level, (swapped, charges, lj_depth, cluster_fill, neighbours, send_lists, couplings))
```

```python
import jax
import jax.numpy as jnp
from jax import lax
from jax.experimental import pallas as pl
from jax.experimental.pallas import tpu as pltpu
from jax.sharding import PartitionSpec as P

STEPS = 2
LANES = 128

time_step = 0.2
softening = 0.5

VMEM = pl.BlockSpec(memory_space=pltpu.VMEM)
SMEM = pl.BlockSpec(memory_space=pltpu.SMEM)
MESH = pl.DeviceIdType.MESH
f32 = jnp.float32
i32 = jnp.int32
bf16 = jnp.bfloat16

WIDE = 256
WIDE_QUADS = 1

POS = 32766.0
Q_STEPS = 8191.0
E_STEPS = 32767.0


def upper_half():
    return lax.broadcasted_iota(i32, (8, LANES), 0) >= 4


def row(values):
    return jnp.broadcast_to(values, (8, LANES))


def twice(tile):
    return jnp.concatenate([tile, tile], 0)


def lookup(tabs, first, count, low, high):
    bits = max(count - 1, 0).bit_length()
    masks = [(high & (1 << b)) != 0 for b in range(bits)]

    def find(tab, bit, start):
        if bit < 0:
            return jnp.take_along_axis(tab[first + start], low, axis=1)
        lower = find(tab, bit - 1, start)
        if start + (1 << bit) >= count:
            return lower
        return jnp.where(masks[bit], find(tab, bit - 1, start + (1 << bit)), lower)

    return [find(tab, bits - 1, 0) for tab in tabs]


def quad_index(near, quad, base):
    rows = [row(near[4 * quad + n : 4 * quad + n + 1, pl.ds(base, LANES)]) for n in range(4)]
    sublane = lax.broadcasted_iota(i32, (8, LANES), 0)
    return jnp.where(
        sublane < 4,
        jnp.where(sublane < 2, rows[0], rows[1]),
        jnp.where(sublane < 6, rows[2], rows[3]),
    )


def two_rows(first, second):
    odd = (lax.broadcasted_iota(i32, (8, LANES), 0) & 1) == 1
    return jnp.where(odd, row(second), row(first))


def low16(word):
    return (word << 16) >> 16


def fill_exact(tab, block):
    for k in range(block.shape[1] // LANES):
        tab[k] = twice(block[:, k * LANES : (k + 1) * LANES])


def gather_ghosts(tab, comps, own, gs, out_first, out_last):
    width = out_first.shape[2]
    up = upper_half()
    for g in range(width // LANES):
        index = jnp.where(
            up,
            row(gs[:, width + g * LANES : width + (g + 1) * LANES]),
            row(gs[:, g * LANES : (g + 1) * LANES]),
        )
        found = lookup([tab.at[c] for c in range(comps)], 0, own, index & (LANES - 1), index >> 7)
        for c in range(comps):
            out_first[c, :, g * LANES : (g + 1) * LANES] = found[c][:4]
            out_last[c, :, g * LANES : (g + 1) * LANES] = found[c][4:]


def pack_params(tabs, first, par):
    for k in range(par.shape[2] // LANES):
        cut = slice(k * LANES, (k + 1) * LANES)
        q = (par[0, :, cut] * Q_STEPS + 32768.5).astype(i32) - 32768
        e = (par[1, :, cut] * E_STEPS + 0.5).astype(i32)
        word = (q << 16) | e
        for half in range(2):
            tabs[half][first + k] = two_rows(word[2 * half : 2 * half + 1], word[2 * half + 1 : 2 * half + 2])


def largest(blocks):
    top = None
    for block in blocks:
        for c in range(3):
            here = jnp.max(jnp.abs(block[c]), axis=0, keepdims=True)
            here = jnp.max(here, axis=1, keepdims=True)
            top = here if top is None else jnp.maximum(top, here)
    return jnp.maximum(top, 1e-30)


def pack_positions(tabs, first, pos, top):
    factor = POS / top
    for k in range(pos.shape[2] // LANES):
        cut = slice(k * LANES, (k + 1) * LANES)
        x, y, z = [(pos[c, :, cut] * factor + 32768.5).astype(i32) - 32768 for c in range(3)]
        word = (x << 16) | (y & 65535)
        depth = (z[0:2] << 16) | (z[2:4] & 65535)
        tabs[0][first + k] = two_rows(word[0:1], word[1:2])
        tabs[1][first + k] = two_rows(word[2:3], word[3:4])
        tabs[2][first + k] = two_rows(depth[0:1], depth[1:2])


def unpack_positions(words, unit):
    third = (words[2] >> 16, low16(words[2]))
    return [
        [v.astype(f32) * unit for v in (words[half] >> 16, low16(words[half]), third[half])]
        for half in range(2)
    ]


def wide_pieces(block, c):
    return [block[c, :, k * WIDE : (k + 1) * WIDE] for k in range(block.shape[2] // WIDE)]


def fill_wide(tab, first, comps, blocks):
    per_comp = tab.shape[1] // comps
    for c in range(comps):
        pieces = [piece for block in blocks for piece in wide_pieces(block, c)]
        for k in range(0, len(pieces), 4):
            stack = jnp.concatenate(pieces[k : k + 4], 0)
            big = stack.astype(bf16)
            rows = pl.ds(c * per_comp + (first + k) * 4, 16)
            tab[0, rows, :] = big
            tab[1, rows, :] = (stack - big.astype(f32)).astype(bf16)


def wide_rows(near, quad, tile, base):
    first = 4 * quad + 2 * tile
    return [near[n : n + 1, pl.ds(base, LANES)] for n in (first, first + 1)]


def one_hot(rows):
    slot = lax.broadcasted_iota(i32, (WIDE, LANES), 0)
    return jnp.concatenate([(slot == (r & (WIDE - 1))).astype(f32).astype(bf16) for r in rows], 1)


def wide_find(tab, comps, weights, rows):
    found = jnp.dot(tab[0], weights, preferred_element_type=f32) + jnp.dot(
        tab[1], weights, preferred_element_type=f32
    )
    pairs = tab.shape[1] // comps // 8
    bits = max(pairs - 1, 0).bit_length()
    up = upper_half()
    highs = [row(r) >> 8 for r in rows]
    masks = [[(high & (2 << b)) != 0 for b in range(bits)] for high in highs]
    even = ((jnp.where(up, highs[1], highs[0]) & 1) == 1) == up

    def choose(c, side, bit, start):
        if bit < 0:
            top = (c * pairs + start) * 8
            return found[top : top + 8, side * LANES : (side + 1) * LANES]
        lower = choose(c, side, bit - 1, start)
        if start + (1 << bit) >= pairs:
            return lower
        return jnp.where(masks[side][bit], choose(c, side, bit - 1, start + (1 << bit)), lower)

    out = []
    for c in range(comps):
        a, b = choose(c, 0, bits - 1, 0), choose(c, 1, bits - 1, 0)
        crossed = pltpu.roll(jnp.where(up, a, b), 4, 0)
        out.append(jnp.where(even, jnp.where(up, b, a), crossed))
    return out


def forces(pos, par, base, found, params):
    lanes = pl.ds(base, LANES)
    force = [[None] * 4 for _ in range(3)]
    for quad in range(len(params)):
        halves = found(quad)
        for half in range(2):
            there = halves[half]
            charge, depth = params[quad][half]
            for i in range(4):
                offset = [row(pos[c, i : i + 1, lanes]) - there[c] for c in range(3)]
                square = offset[0] * offset[0] + offset[1] * offset[1] + offset[2] * offset[2]
                root = lax.rsqrt(square + softening)
                w = root * root
                qq = row(par[0, i : i + 1, lanes]) * charge
                ee = row(par[1, i : i + 1, lanes]) * depth
                weight = w * (qq * root + ee * (w * w - w))
                for c in range(3):
                    term = weight * offset[c]
                    force[c][i] = term if quad + half == 0 else force[c][i] + term
    return [
        jnp.concatenate([jnp.sum(force[c][i], axis=0, keepdims=True) for i in range(4)], 0)
        for c in range(3)
    ]


def kernel(
    partner, scale_order, coupling, phase, charges, lj, fill, near, gs, out,
    from_low, from_high, par, par_first, par_last, par_low, par_high,
    pos_first, pos_last, pos_low, pos_high, pos, pos_next, vel,
    exact, packed_par, packed_pos, gathered, part, part_par, wide_par, wide_pos, hot, send_sem, recv_sem,
):
    total, width = phase.shape[2], gs.shape[1] // 2
    own, ghost = total // LANES, width // LANES
    tiles = own + 2 * ghost
    early = own // 4
    quads = near.shape[0] // 4
    slim = quads - WIDE_QUADS
    level, levels = lax.axis_index("rep"), lax.axis_size("rep")
    place, places = lax.axis_index("space"), lax.axis_size("space")
    has_low, has_high = level > 0, level < levels - 1
    above, below = lax.rem(place + 1, places), lax.rem(place + places - 1, places)

    barrier = pltpu.get_barrier_semaphore()

    def greet(device):
        pl.semaphore_signal(barrier, inc=1, device_id=device, device_id_type=MESH)

    greet({"space": above})
    greet({"space": below})

    @pl.when(has_low)
    def _():
        greet({"rep": level - 1})

    @pl.when(has_high)
    def _():
        greet({"rep": level + 1})

    def remote(src, dst, number, device):
        return pltpu.make_async_remote_copy(
            src_ref=src, dst_ref=dst, send_sem=send_sem.at[number], recv_sem=recv_sem.at[number],
            device_id=device, device_id_type=MESH,
        )

    def ring(first, last, low, high, number):
        return [remote(last, low, number, {"space": above}), remote(first, high, number + 1, {"space": below})]

    def each_group(start, stop, body):
        def step(group, carry):
            body(group, pl.multiple_of(group * LANES, LANES))
            return carry

        lax.fori_loop(start, stop, step, 0, unroll=2)

    slot = lax.broadcasted_iota(i32, (4, total), 0)
    present = (slot < fill[...]).astype(f32)
    par[0] = charges[...] * present
    par[1] = lj[...] * present
    for c in range(2):
        fill_exact(exact.at[c], par[c])
    gather_ghosts(exact, 2, own, gs, par_first, par_last)
    par_tabs = [packed_par.at[0], packed_par.at[1]]
    pack_params(par_tabs, 0, par)
    fill_wide(wide_par, 0, 2, [par])

    def look_ahead(tabs, kept, group, base):
        for quad in range(slim):
            index = quad_index(near, quad, base)
            for n, word in enumerate(lookup(tabs, 0, own, index & (LANES - 1), index >> 7)):
                kept[group, quad, n] = word

    def params_ahead(group, base):
        look_ahead(par_tabs, part_par, group, base)
        for quad in range(slim, quads):
            for tile in range(2):
                hot[group, quad - slim, tile] = one_hot(wide_rows(near, quad, tile, base))

    each_group(0, early, params_ahead)

    pl.semaphore_wait(barrier, 2 + jnp.where(has_low, 1, 0) + jnp.where(has_high, 1, 0))

    halves = (pl.ds(0, 3), pl.ds(3, 3))
    rising = [remote(phase.at[h], from_low.at[h], n, {"rep": level + 1}) for n, h in enumerate(halves)]
    falling = [remote(phase.at[h], from_high.at[h], 2 + n, {"rep": level - 1}) for n, h in enumerate(halves)]

    def swap_start(n):
        @pl.when(has_high)
        def _():
            rising[n].start()

        @pl.when(has_low)
        def _():
            falling[n].start()

    def swap_arrived(n):
        @pl.when(has_low)
        def _():
            rising[n].wait_recv()

        @pl.when(has_high)
        def _():
            falling[n].wait_recv()

    swap_start(0)
    par_ring = ring(par_first, par_last, par_low, par_high, 4)
    for copy in par_ring:
        copy.start()
    swap_start(1)

    each_group(early, own, params_ahead)

    def find_rest(tabs, kept, group, quad, index):
        words = lookup(tabs, own, tiles - own, index & (LANES - 1), (index >> 7) - own)
        return [jnp.where(index < total, kept[group, quad, n], word) for n, word in enumerate(words)]

    moved = partner[level] - level

    def swapped(c, lanes):
        return jnp.where(
            moved == 0, phase[c, :, lanes],
            jnp.where(moved < 0, from_low[c, :, lanes], from_high[c, :, lanes]),
        )

    swap_arrived(0)
    for c in range(3):
        block = swapped(c, pl.ds(0, total))
        pos[c] = block
        fill_exact(exact.at[c], block)
    gather_ghosts(exact, 3, own, gs, pos_first.at[0], pos_last.at[0])
    pos_rings = [
        ring(pos_first.at[n], pos_last.at[n], pos_low.at[n], pos_high.at[n], 6 + 2 * n) for n in range(2)
    ]
    for copy in pos_rings[0]:
        copy.start()
    tabs = [packed_pos.at[n] for n in range(3)]
    top_own = largest([pos])
    pack_positions(tabs, 0, pos, top_own)
    fill_wide(wide_pos, 0, 3, [pos])
    unit_own = top_own * (1.0 / POS)

    for copy in par_ring:
        copy.wait_recv()
    pack_params(par_tabs, own, par_low)
    pack_params(par_tabs, own + ghost, par_high)
    wide_own = total // WIDE
    fill_wide(wide_par, wide_own, 2, [par_low, par_high])
    strength = coupling[scale_order[level]]

    def finish_params(group, base):
        look_ahead(tabs, part, group, base)
        for quad in range(slim):
            words = find_rest(par_tabs, part_par, group, quad, quad_index(near, quad, base))
            for half, word in enumerate(words):
                gathered[group, quad, half, 0] = (word >> 16).astype(f32) * (strength * (1.0 / Q_STEPS))
                gathered[group, quad, half, 1] = (word & 65535).astype(f32) * (1.0 / E_STEPS)
        for quad in range(slim, quads):
            for tile in range(2):
                rows = wide_rows(near, quad, tile, base)
                charge, depth = wide_find(wide_par, 2, hot[group, quad - slim, tile], rows)
                gathered[group, quad, tile, 0] = charge * strength
                gathered[group, quad, tile, 1] = depth

    each_group(0, own, finish_params)

    def ghosts_arrived(n):
        for copy in pos_rings[n]:
            copy.wait_recv()
        low, high = pos_low.at[n], pos_high.at[n]
        top = largest([low, high])
        pack_positions(tabs, own, low, top)
        pack_positions(tabs, own + ghost, high, top)
        fill_wide(wide_pos, wide_own, 3, [low, high])
        return top * (1.0 / POS)

    def params_of(group):
        return [
            [(gathered[group, quad, half, 0], gathered[group, quad, half, 1]) for half in range(2)]
            for quad in range(quads)
        ]

    def finder(group, base, unit_here, unit_there):
        def found(quad):
            if quad >= slim:
                return [
                    wide_find(wide_pos, 3, hot[group, quad - slim, tile], wide_rows(near, quad, tile, base))
                    for tile in range(2)
                ]
            index = quad_index(near, quad, base)
            words = find_rest(tabs, part, group, quad, index)
            return unpack_positions(words, jnp.where(index < total, unit_here, unit_there))

        return found

    swap_arrived(1)
    unit_ghost = ghosts_arrived(0)

    def first_step(group, base):
        lanes = pl.ds(base, LANES)
        force = forces(pos, par, base, finder(group, base, unit_own, unit_ghost), params_of(group))
        for c in range(3):
            v = swapped(3 + c, lanes) + time_step * force[c]
            vel[c, :, lanes] = v
            pos_next[c, :, lanes] = pos[c, :, lanes] + time_step * v

    each_group(0, own, first_step)

    for c in range(3):
        fill_exact(exact.at[c], pos_next[c])
    gather_ghosts(exact, 3, own, gs, pos_first.at[1], pos_last.at[1])
    for copy in pos_rings[1]:
        copy.start()
    top_own = largest([pos_next])
    pack_positions(tabs, 0, pos_next, top_own)
    fill_wide(wide_pos, 0, 3, [pos_next])
    unit_own_next = top_own * (1.0 / POS)

    each_group(0, own, lambda group, base: look_ahead(tabs, part, group, base))
    unit_ghost_next = ghosts_arrived(1)

    def second_step(group, base):
        lanes = pl.ds(base, LANES)
        found = finder(group, base, unit_own_next, unit_ghost_next)
        force = forces(pos_next, par, base, found, params_of(group))
        for c in range(3):
            v = vel[c, :, lanes] + time_step * force[c]
            out[3 + c, :, lanes] = v
            out[c, :, lanes] = pos_next[c, :, lanes] + time_step * v

    each_group(0, own, second_step)

    for copy in par_ring + pos_rings[0] + pos_rings[1]:
        copy.wait_send()
    for n in range(2):

        @pl.when(has_high)
        def _():
            rising[n].wait_send()

        @pl.when(has_low)
        def _():
            falling[n].wait_send()


def on_device(
    phase_space, charges, lj_depth, cluster_fill, neighbours, ghost_send, partner, scale_order, coupling
):
    phase = phase_space[0]
    rows, slots, total = phase.shape
    width = ghost_send.shape[1] // 2
    own = total // LANES
    tiles = own + 2 * (width // LANES)
    quads = neighbours.shape[1] // 4
    wides = tiles * LANES // WIDE
    out = pl.pallas_call(
        kernel,
        out_shape=jax.ShapeDtypeStruct(phase.shape, f32),
        in_specs=[SMEM] * 3 + [VMEM] * 6,
        out_specs=VMEM,
        scratch_shapes=[
            pltpu.VMEM((rows, slots, total), f32),
            pltpu.VMEM((rows, slots, total), f32),
            pltpu.VMEM((2, slots, total), f32),
        ]
        + [pltpu.VMEM((2, slots, width), f32)] * 4
        + [pltpu.VMEM((2, 3, slots, width), f32)] * 4
        + [pltpu.VMEM((3, slots, total), f32)] * 3
        + [
            pltpu.VMEM((3, own, 8, LANES), f32),
            pltpu.VMEM((2, tiles, 8, LANES), i32),
            pltpu.VMEM((3, tiles, 8, LANES), i32),
            pltpu.VMEM((own, quads, 2, 2, 8, LANES), f32),
            pltpu.VMEM((own, quads - WIDE_QUADS, 3, 8, LANES), i32),
            pltpu.VMEM((own, quads - WIDE_QUADS, 2, 8, LANES), i32),
            pltpu.VMEM((2, 2 * 4 * wides, WIDE), bf16),
            pltpu.VMEM((2, 3 * 4 * wides, WIDE), bf16),
            pltpu.VMEM((own, WIDE_QUADS, 2, WIDE, 2 * LANES), bf16),
            pltpu.SemaphoreType.DMA((10,)),
            pltpu.SemaphoreType.DMA((10,)),
        ],
        compiler_params=pltpu.CompilerParams(collective_id=0, has_side_effects=True),
    )(partner, scale_order, coupling, phase, charges[0], lj_depth[0], cluster_fill, neighbours[0], ghost_send)
    return out[None]


def solution(mesh):
    return jax.shard_map(
        on_device,
        mesh=mesh,
        in_specs=(
            P("rep", None, None, "space"),
            P("rep", None, "space"),
            P("rep", None, "space"),
            P("rep", "space"),
            P("rep", None, "space"),
            P("rep", "space"),
            P(),
            P(),
            P(),
        ),
        out_specs=P("rep", None, None, "space"),
        check_vma=False,
    )
```

```python
import jax
import jax.numpy as jnp
from jax import lax
from jax.experimental import pallas as pl
from jax.experimental.pallas import tpu as pltpu
from jax.sharding import PartitionSpec as P

STEPS = 2
LANES = 128

time_step = 0.2
softening = 0.5

VMEM = pl.BlockSpec(memory_space=pltpu.VMEM)
MESH = pl.DeviceIdType.MESH
f32 = jnp.float32
i32 = jnp.int32
bf16 = jnp.bfloat16

WIDE = 256
WIDE_QUADS = 1

POS = 32766.0
UNIT = 1.0 / (POS * 65536)
Q_STEPS = 8191.0
E_STEPS = 32767.0


def upper_half():
    return lax.broadcasted_iota(i32, (8, LANES), 0) >= 4


def row(values):
    return jnp.broadcast_to(values, (8, LANES))


def twice(tile):
    return jnp.concatenate([tile, tile], 0)


def lookup(tabs, first, count, low, high):
    bits = max(count - 1, 0).bit_length()
    masks = [(high & (1 << b)) != 0 for b in range(bits)]

    def find(tab, bit, start):
        if bit < 0:
            return jnp.take_along_axis(tab[first + start], low, axis=1)
        lower = find(tab, bit - 1, start)
        if start + (1 << bit) >= count:
            return lower
        return jnp.where(masks[bit], find(tab, bit - 1, start + (1 << bit)), lower)

    return [find(tab, bits - 1, 0) for tab in tabs]


def quad_index(near, quad, base):
    rows = [row(near[4 * quad + n : 4 * quad + n + 1, pl.ds(base, LANES)]) for n in range(4)]
    sublane = lax.broadcasted_iota(i32, (8, LANES), 0)
    return jnp.where(
        sublane < 4,
        jnp.where(sublane < 2, rows[0], rows[1]),
        jnp.where(sublane < 6, rows[2], rows[3]),
    )


def two_rows(first, second):
    odd = (lax.broadcasted_iota(i32, (8, LANES), 0) & 1) == 1
    return jnp.where(odd, row(second), row(first))


def low16(word):
    return (word << 16) >> 16


def fill_exact(tab, block):
    for k in range(block.shape[1] // LANES):
        tab[k] = twice(block[:, k * LANES : (k + 1) * LANES])


def gather_ghosts(tab, comps, own, gs, out_first, out_last):
    width = out_first.shape[2]
    up = upper_half()
    for g in range(width // LANES):
        index = jnp.where(
            up,
            row(gs[:, width + g * LANES : width + (g + 1) * LANES]),
            row(gs[:, g * LANES : (g + 1) * LANES]),
        )
        found = lookup([tab.at[c] for c in range(comps)], 0, own, index & (LANES - 1), index >> 7)
        for c in range(comps):
            out_first[c, :, g * LANES : (g + 1) * LANES] = found[c][:4]
            out_last[c, :, g * LANES : (g + 1) * LANES] = found[c][4:]


def pack_params(tabs, first, par):
    for k in range(par.shape[2] // LANES):
        cut = slice(k * LANES, (k + 1) * LANES)
        q = (par[0, :, cut] * Q_STEPS + 32768.5).astype(i32) - 32768
        e = (par[1, :, cut] * E_STEPS + 0.5).astype(i32)
        word = (q << 16) | e
        for half in range(2):
            tabs[half][first + k] = two_rows(word[2 * half : 2 * half + 1], word[2 * half + 1 : 2 * half + 2])


def largest(blocks):
    top = None
    for block in blocks:
        for c in range(3):
            here = jnp.max(jnp.abs(block[c]), axis=0, keepdims=True)
            here = jnp.max(here, axis=1, keepdims=True)
            top = here if top is None else jnp.maximum(top, here)
    return jnp.maximum(top, 1e-30)


def both_halves(high, low):
    low = ((low + 32768.5).astype(i32) - 32768) & 65535
    high = (high + 32768.5 - low.astype(f32) * (1.0 / 65536)).astype(i32) - 32768
    return (high << 16) | low


def pack_positions(tabs, first, pos, top):
    factor = POS / top
    for k in range(pos.shape[2] // LANES):
        cut = slice(k * LANES, (k + 1) * LANES)
        x, y, z = [pos[c, :, cut] * factor for c in range(3)]
        word = both_halves(x, y)
        depth = both_halves(z[0:2], z[2:4])
        tabs[0][first + k] = two_rows(word[0:1], word[1:2])
        tabs[1][first + k] = two_rows(word[2:3], word[3:4])
        tabs[2][first + k] = two_rows(depth[0:1], depth[1:2])


def unpack_positions(words, unit):
    third = (words[2], words[2] << 16)
    return [
        [v.astype(f32) * unit for v in (words[half], words[half] << 16, third[half])] for half in range(2)
    ]


def wide_pieces(block, c):
    return [block[c, :, k * WIDE : (k + 1) * WIDE] for k in range(block.shape[2] // WIDE)]


def fill_wide(tab, first, comps, blocks):
    per_comp = tab.shape[1] // comps
    for c in range(comps):
        pieces = [piece for block in blocks for piece in wide_pieces(block, c)]
        for k in range(0, len(pieces), 4):
            stack = jnp.concatenate(pieces[k : k + 4], 0)
            big = stack.astype(bf16)
            rows = pl.ds(c * per_comp + (first + k) * 4, 16)
            tab[0, rows, :] = big
            tab[1, rows, :] = (stack - big.astype(f32)).astype(bf16)


def wide_rows(near, quad, tile, base):
    first = 4 * quad + 2 * tile
    return [near[n : n + 1, pl.ds(base, LANES)] for n in (first, first + 1)]


def one_hot(rows):
    slot = lax.broadcasted_iota(i32, (WIDE, LANES), 0)
    return jnp.concatenate([(slot == (r & (WIDE - 1))).astype(f32).astype(bf16) for r in rows], 1)


def wide_find(tab, comps, weights, rows):
    found = jnp.dot(tab[0], weights, preferred_element_type=f32) + jnp.dot(
        tab[1], weights, preferred_element_type=f32
    )
    pairs = tab.shape[1] // comps // 8
    bits = max(pairs - 1, 0).bit_length()
    up = upper_half()
    highs = [row(r) >> 8 for r in rows]
    masks = [[(high & (2 << b)) != 0 for b in range(bits)] for high in highs]
    even = ((jnp.where(up, highs[1], highs[0]) & 1) == 1) == up

    def choose(c, side, bit, start):
        if bit < 0:
            top = (c * pairs + start) * 8
            return found[top : top + 8, side * LANES : (side + 1) * LANES]
        lower = choose(c, side, bit - 1, start)
        if start + (1 << bit) >= pairs:
            return lower
        return jnp.where(masks[side][bit], choose(c, side, bit - 1, start + (1 << bit)), lower)

    out = []
    for c in range(comps):
        a, b = choose(c, 0, bits - 1, 0), choose(c, 1, bits - 1, 0)
        crossed = pltpu.roll(jnp.where(up, a, b), 4, 0)
        out.append(jnp.where(even, jnp.where(up, b, a), crossed))
    return out


def fold(parts):
    sublane = lax.broadcasted_iota(i32, (8, LANES), 0)
    up, second = sublane >= 4, (sublane & 2) != 0
    outer = [
        jnp.where(up, b, a) + pltpu.roll(jnp.where(up, a, b), 4, 0)
        for a, b in ((parts[0], parts[2]), (parts[1], parts[3]))
    ]
    swapped = jnp.take_along_axis(jnp.where(second, outer[0], outer[1]), sublane ^ 2, axis=0)
    inner = jnp.where(second, outer[1], outer[0]) + swapped
    even = (sublane * 2) & 7
    both = jnp.take_along_axis(inner, even, axis=0) + jnp.take_along_axis(inner, even + 1, axis=0)
    return both[:4]


def forces(pos, ratio, lanes, there, params, quads):
    force = [[None] * 4 for _ in range(3)]
    for quad in range(quads):
        for half in range(2):
            other = [there[quad, half, c] for c in range(3)]
            charge, depth = params[quad, half, 0], params[quad, half, 1]
            for i in range(4):
                offset = [row(pos[c, i : i + 1, lanes]) - other[c] for c in range(3)]
                square = offset[0] * offset[0] + (offset[1] * offset[1] + (offset[2] * offset[2] + softening))
                root = lax.rsqrt(square)
                w = root * root
                weight = w * (row(ratio[i : i + 1, lanes]) * charge * root + depth * ((w - 1.0) * w))
                for c in range(3):
                    term = weight * offset[c]
                    force[c][i] = term if quad + half == 0 else force[c][i] + term
    return [fold(force[c]) for c in range(3)]


def kernel(
    partner_in, order_in, coupling_in, phase_in, charges_in, lj_in, fill_in, near_in, gs_in, out,
    partner, scale_order, coupling, phase, charges, lj, fill, near, gs, ratio, spot_even, spot_odd,
    from_low, from_high, par, par_first, par_last, par_low, par_high,
    pos_first, pos_last, pos_low, pos_high, pos, pos_next, vel,
    exact, packed_par, packed_pos, gathered, part, part_par, wide_par, wide_pos, hot, load_sem, send_sem, recv_sem,
):
    total, width = phase.shape[2], gs.shape[1] // 2
    own, ghost = total // LANES, width // LANES
    tiles = own + 2 * ghost
    early = own // 4
    quads = near.shape[0] // 4
    slim = quads - WIDE_QUADS
    level, levels = lax.axis_index("rep"), lax.axis_size("rep")
    place, places = lax.axis_index("space"), lax.axis_size("space")
    has_low, has_high = level > 0, level < levels - 1
    above, below = lax.rem(place + 1, places), lax.rem(place + places - 1, places)

    barrier = pltpu.get_barrier_semaphore()

    def greet(device):
        pl.semaphore_signal(barrier, inc=1, device_id=device, device_id_type=MESH)

    greet({"space": above})
    greet({"space": below})

    @pl.when(has_low)
    def _():
        greet({"rep": level - 1})

    @pl.when(has_high)
    def _():
        greet({"rep": level + 1})

    loads = [
        pltpu.make_async_copy(src, dst, load_sem.at[n])
        for n, (src, dst) in enumerate(
            [
                (fill_in, fill), (charges_in, charges), (lj_in, lj), (gs_in, gs), (near_in, near),
                (phase_in, phase), (partner_in, partner), (order_in, scale_order), (coupling_in, coupling),
            ]
        )
    ]
    for copy in loads:
        copy.start()

    def remote(src, dst, number, device):
        return pltpu.make_async_remote_copy(
            src_ref=src, dst_ref=dst, send_sem=send_sem.at[number], recv_sem=recv_sem.at[number],
            device_id=device, device_id_type=MESH,
        )

    def ring(first, last, low, high, number):
        return [remote(last, low, number, {"space": above}), remote(first, high, number + 1, {"space": below})]

    def each_group(start, stop, body):
        def step(group, carry):
            body(group, pl.multiple_of(group * LANES, LANES))
            return carry

        lax.fori_loop(start, stop, step, 0, unroll=2)

    for copy in loads[:4]:
        copy.wait()
    slot = lax.broadcasted_iota(i32, (4, total), 0)
    present = (slot < fill[...]).astype(f32)
    par[0] = charges[...] * present
    par[1] = lj[...] * present
    ratio[...] = charges[...] / lj[...]
    for c in range(2):
        fill_exact(exact.at[c], par[c])
    gather_ghosts(exact, 2, own, gs, par_first, par_last)
    par_tabs = [packed_par.at[0], packed_par.at[1]]
    pack_params(par_tabs, 0, par)
    fill_wide(wide_par, 0, 2, [par])

    def look_ahead(tabs, kept, group, base):
        for quad in range(slim):
            index = quad_index(near, quad, base)
            for n, word in enumerate(lookup(tabs, 0, own, index & (LANES - 1), index >> 7)):
                kept[group, quad, n] = word

    def params_ahead(group, base):
        look_ahead(par_tabs, part_par, group, base)
        for quad in range(slim, quads):
            for tile in range(2):
                hot[group, quad - slim, tile] = one_hot(wide_rows(near, quad, tile, base))

    for copy in loads[4:]:
        copy.wait()
    each_group(0, early, params_ahead)

    pl.semaphore_wait(barrier, 2 + jnp.where(has_low, 1, 0) + jnp.where(has_high, 1, 0))

    halves = (pl.ds(0, 3), pl.ds(3, 3))
    rising = [remote(phase.at[h], from_low.at[h], n, {"rep": level + 1}) for n, h in enumerate(halves)]
    falling = [remote(phase.at[h], from_high.at[h], 2 + n, {"rep": level - 1}) for n, h in enumerate(halves)]

    def swap_start(n):
        @pl.when(has_high)
        def _():
            rising[n].start()

        @pl.when(has_low)
        def _():
            falling[n].start()

    def swap_arrived(n):
        @pl.when(has_low)
        def _():
            rising[n].wait_recv()

        @pl.when(has_high)
        def _():
            falling[n].wait_recv()

    swap_start(0)
    par_ring = ring(par_first, par_last, par_low, par_high, 4)
    for copy in par_ring:
        copy.start()
    swap_start(1)

    each_group(early, own, params_ahead)

    def find_rest(tabs, kept, group, quad, index):
        words = lookup(tabs, own, tiles - own, index & (LANES - 1), (index >> 7) - own)
        return [jnp.where(index < total, kept[group, quad, n], word) for n, word in enumerate(words)]

    moved = partner[level] - level

    def swapped(c, lanes):
        return jnp.where(
            moved == 0, phase[c, :, lanes],
            jnp.where(moved < 0, from_low[c, :, lanes], from_high[c, :, lanes]),
        )

    swap_arrived(0)
    for c in range(3):
        block = swapped(c, pl.ds(0, total))
        pos[c] = block
        fill_exact(exact.at[c], block)
    gather_ghosts(exact, 3, own, gs, pos_first.at[0], pos_last.at[0])
    pos_rings = [
        ring(pos_first.at[n], pos_last.at[n], pos_low.at[n], pos_high.at[n], 6 + 2 * n) for n in range(2)
    ]
    for copy in pos_rings[0]:
        copy.start()
    tabs = [packed_pos.at[n] for n in range(3)]
    top_own = largest([pos])
    pack_positions(tabs, 0, pos, top_own)
    fill_wide(wide_pos, 0, 3, [pos])
    unit_own = top_own * UNIT

    for copy in par_ring:
        copy.wait_recv()
    pack_params(par_tabs, own, par_low)
    pack_params(par_tabs, own + ghost, par_high)
    wide_own = total // WIDE
    fill_wide(wide_par, wide_own, 2, [par_low, par_high])
    strength = coupling[scale_order[level]]

    def finish_params(group, base):
        look_ahead(tabs, part, group, base)
        for quad in range(slim):
            words = find_rest(par_tabs, part_par, group, quad, quad_index(near, quad, base))
            for half, word in enumerate(words):
                gathered[group, quad, half, 0] = (word >> 16).astype(f32) * (strength * (1.0 / Q_STEPS))
                gathered[group, quad, half, 1] = (word & 65535).astype(f32) * (1.0 / E_STEPS)
        for quad in range(slim, quads):
            for tile in range(2):
                rows = wide_rows(near, quad, tile, base)
                charge, depth = wide_find(wide_par, 2, hot[group, quad - slim, tile], rows)
                gathered[group, quad, tile, 0] = charge * strength
                gathered[group, quad, tile, 1] = depth

    each_group(0, own, finish_params)

    def ghosts_arrived(n):
        for copy in pos_rings[n]:
            copy.wait_recv()
        low, high = pos_low.at[n], pos_high.at[n]
        top = largest([low, high])
        pack_positions(tabs, own, low, top)
        pack_positions(tabs, own + ghost, high, top)
        fill_wide(wide_pos, wide_own, 3, [low, high])
        return top * UNIT

    def find(group, spot, unit_here, unit_there):
        base = pl.multiple_of(group * LANES, LANES)
        for quad in range(quads):
            if quad < slim:
                index = quad_index(near, quad, base)
                words = find_rest(tabs, part, group, quad, index)
                pair = unpack_positions(words, jnp.where(index < total, unit_here, unit_there))
            else:
                pair = [
                    wide_find(wide_pos, 3, hot[group, quad - slim, tile], wide_rows(near, quad, tile, base))
                    for tile in range(2)
                ]
            for half in range(2):
                for c in range(3):
                    spot[quad, half, c] = pair[half][c]

    def move_all(move, unit_here, unit_there):
        find(0, spot_even, unit_here, unit_there)

        def step(couple, carry):
            group = 2 * couple
            move(group, spot_even)
            find(group + 1, spot_odd, unit_here, unit_there)
            move(group + 1, spot_odd)
            find(jnp.minimum(group + 2, own - 1), spot_even, unit_here, unit_there)
            return carry

        lax.fori_loop(0, own // 2, step, 0)

    def force_on(where, group, spot):
        lanes = pl.ds(pl.multiple_of(group * LANES, LANES), LANES)
        depth = par[1, :, lanes]
        return lanes, [f * depth for f in forces(where, ratio, lanes, spot, gathered.at[group], quads)]

    swap_arrived(1)
    unit_ghost = ghosts_arrived(0)

    def first_step(group, spot):
        lanes, force = force_on(pos, group, spot)
        for c in range(3):
            v = swapped(3 + c, lanes) + time_step * force[c]
            vel[c, :, lanes] = v
            pos_next[c, :, lanes] = pos[c, :, lanes] + time_step * v

    move_all(first_step, unit_own, unit_ghost)

    for c in range(3):
        fill_exact(exact.at[c], pos_next[c])
    gather_ghosts(exact, 3, own, gs, pos_first.at[1], pos_last.at[1])
    for copy in pos_rings[1]:
        copy.start()
    top_own = largest([pos_next])
    pack_positions(tabs, 0, pos_next, top_own)
    fill_wide(wide_pos, 0, 3, [pos_next])
    unit_own_next = top_own * UNIT

    each_group(0, own, lambda group, base: look_ahead(tabs, part, group, base))
    unit_ghost_next = ghosts_arrived(1)

    def second_step(group, spot):
        lanes, force = force_on(pos_next, group, spot)
        for c in range(3):
            v = vel[c, :, lanes] + time_step * force[c]
            out[3 + c, :, lanes] = v
            out[c, :, lanes] = pos_next[c, :, lanes] + time_step * v

    move_all(second_step, unit_own_next, unit_ghost_next)

    for copy in par_ring + pos_rings[0] + pos_rings[1]:
        copy.wait_send()
    for n in range(2):

        @pl.when(has_high)
        def _():
            rising[n].wait_send()

        @pl.when(has_low)
        def _():
            falling[n].wait_send()


def on_device(
    phase_space, charges, lj_depth, cluster_fill, neighbours, ghost_send, partner, scale_order, coupling
):
    phase = phase_space[0]
    rows, slots, total = phase.shape
    width = ghost_send.shape[1] // 2
    own = total // LANES
    tiles = own + 2 * (width // LANES)
    quads = neighbours.shape[1] // 4
    wides = tiles * LANES // WIDE
    out = pl.pallas_call(
        kernel,
        out_shape=pltpu.VMEM(phase.shape, f32),
        in_specs=[pl.BlockSpec(memory_space=pltpu.HBM)] * 9,
        out_specs=VMEM,
        scratch_shapes=[
            pltpu.SMEM(partner.shape, i32),
            pltpu.SMEM(scale_order.shape, i32),
            pltpu.SMEM(coupling.shape, f32),
            pltpu.VMEM((rows, slots, total), f32),
            pltpu.VMEM((slots, total), f32),
            pltpu.VMEM((slots, total), f32),
            pltpu.VMEM((1, total), i32),
            pltpu.VMEM((4 * quads, total), i32),
            pltpu.VMEM((1, 2 * width), i32),
            pltpu.VMEM((slots, total), f32),
            pltpu.VMEM((quads, 2, 3, 8, LANES), f32),
            pltpu.VMEM((quads, 2, 3, 8, LANES), f32),
            pltpu.VMEM((rows, slots, total), f32),
            pltpu.VMEM((rows, slots, total), f32),
            pltpu.VMEM((2, slots, total), f32),
        ]
        + [pltpu.VMEM((2, slots, width), f32)] * 4
        + [pltpu.VMEM((2, 3, slots, width), f32)] * 4
        + [pltpu.VMEM((3, slots, total), f32)] * 3
        + [
            pltpu.VMEM((3, own, 8, LANES), f32),
            pltpu.VMEM((2, tiles, 8, LANES), i32),
            pltpu.VMEM((3, tiles, 8, LANES), i32),
            pltpu.VMEM((own, quads, 2, 2, 8, LANES), f32),
            pltpu.VMEM((own, quads - WIDE_QUADS, 3, 8, LANES), i32),
            pltpu.VMEM((own, quads - WIDE_QUADS, 2, 8, LANES), i32),
            pltpu.VMEM((2, 2 * 4 * wides, WIDE), bf16),
            pltpu.VMEM((2, 3 * 4 * wides, WIDE), bf16),
            pltpu.VMEM((own, WIDE_QUADS, 2, WIDE, 2 * LANES), bf16),
            pltpu.SemaphoreType.DMA((9,)),
            pltpu.SemaphoreType.DMA((10,)),
            pltpu.SemaphoreType.DMA((10,)),
        ],
        compiler_params=pltpu.CompilerParams(collective_id=0, has_side_effects=True),
    )(partner, scale_order, coupling, phase, charges[0], lj_depth[0], cluster_fill, neighbours[0], ghost_send)
    return out[None]


def solution(mesh):
    return jax.shard_map(
        on_device,
        mesh=mesh,
        in_specs=(
            P("rep", None, None, "space"),
            P("rep", None, "space"),
            P("rep", None, "space"),
            P("rep", "space"),
            P("rep", None, "space"),
            P("rep", "space"),
            P(),
            P(),
            P(),
        ),
        out_specs=P("rep", None, None, "space"),
        check_vma=False,
    )
```

```python
import jax
import jax.numpy as jnp
from jax import lax
from jax.experimental import pallas as pl
from jax.experimental.pallas import tpu as pltpu
from jax.sharding import PartitionSpec as P

STEPS = 2
LANES = 128

time_step = 0.2
softening = 0.5

VMEM = pl.BlockSpec(memory_space=pltpu.VMEM)
MESH = pl.DeviceIdType.MESH
f32 = jnp.float32
i32 = jnp.int32
bf16 = jnp.bfloat16

WIDE = 256
WIDE_QUADS = 1

POS = 32766.0
UNIT = 1.0 / (POS * 65536)
Q_STEPS = 8191.0
E_STEPS = 32767.0


def upper_half():
    return lax.broadcasted_iota(i32, (8, LANES), 0) >= 4


def row(values):
    return jnp.broadcast_to(values, (8, LANES))


def twice(tile):
    return jnp.concatenate([tile, tile], 0)


def lookup(tabs, first, count, low, high):
    bits = max(count - 1, 0).bit_length()
    masks = [(high & (1 << b)) != 0 for b in range(bits)]

    def find(tab, bit, start):
        if bit < 0:
            return jnp.take_along_axis(tab[first + start], low, axis=1)
        lower = find(tab, bit - 1, start)
        if start + (1 << bit) >= count:
            return lower
        return jnp.where(masks[bit], find(tab, bit - 1, start + (1 << bit)), lower)

    return [find(tab, bits - 1, 0) for tab in tabs]


def quad_index(near, quad, base):
    rows = [row(near[4 * quad + n : 4 * quad + n + 1, pl.ds(base, LANES)]) for n in range(4)]
    sublane = lax.broadcasted_iota(i32, (8, LANES), 0)
    return jnp.where(
        sublane < 4,
        jnp.where(sublane < 2, rows[0], rows[1]),
        jnp.where(sublane < 6, rows[2], rows[3]),
    )


def two_rows(first, second):
    odd = (lax.broadcasted_iota(i32, (8, LANES), 0) & 1) == 1
    return jnp.where(odd, row(second), row(first))


def low16(word):
    return (word << 16) >> 16


def fill_exact(tab, block):
    for k in range(block.shape[1] // LANES):
        tab[k] = twice(block[:, k * LANES : (k + 1) * LANES])


def gather_ghosts(tab, comps, own, gs, out_first, out_last):
    width = out_first.shape[2]
    up = upper_half()
    for g in range(width // LANES):
        index = jnp.where(
            up,
            row(gs[:, width + g * LANES : width + (g + 1) * LANES]),
            row(gs[:, g * LANES : (g + 1) * LANES]),
        )
        found = lookup([tab.at[c] for c in range(comps)], 0, own, index & (LANES - 1), index >> 7)
        for c in range(comps):
            out_first[c, :, g * LANES : (g + 1) * LANES] = found[c][:4]
            out_last[c, :, g * LANES : (g + 1) * LANES] = found[c][4:]


def pack_params(tabs, first, par):
    for k in range(par.shape[2] // LANES):
        cut = slice(k * LANES, (k + 1) * LANES)
        q = (par[0, :, cut] * Q_STEPS + 32768.5).astype(i32) - 32768
        e = (par[1, :, cut] * E_STEPS + 0.5).astype(i32)
        word = (q << 16) | e
        for half in range(2):
            tabs[half][first + k] = two_rows(word[2 * half : 2 * half + 1], word[2 * half + 1 : 2 * half + 2])


def largest(blocks):
    top = None
    for block in blocks:
        for c in range(3):
            here = jnp.max(jnp.abs(block[c]), axis=0, keepdims=True)
            here = jnp.max(here, axis=1, keepdims=True)
            top = here if top is None else jnp.maximum(top, here)
    return jnp.maximum(top, 1e-30)


def both_halves(high, low):
    low = ((low + 32768.5).astype(i32) - 32768) & 65535
    high = (high + 32768.5 - low.astype(f32) * (1.0 / 65536)).astype(i32) - 32768
    return (high << 16) | low


def pack_positions(tabs, first, pos, top):
    factor = POS / top
    for k in range(pos.shape[2] // LANES):
        cut = slice(k * LANES, (k + 1) * LANES)
        x, y, z = [pos[c, :, cut] * factor for c in range(3)]
        word = both_halves(x, y)
        depth = both_halves(z[0:2], z[2:4])
        tabs[0][first + k] = two_rows(word[0:1], word[1:2])
        tabs[1][first + k] = two_rows(word[2:3], word[3:4])
        tabs[2][first + k] = two_rows(depth[0:1], depth[1:2])


def unpack_positions(words, unit):
    third = (words[2], words[2] << 16)
    return [
        [v.astype(f32) * unit for v in (words[half], words[half] << 16, third[half])] for half in range(2)
    ]


def wide_pieces(block, c):
    return [block[c, :, k * WIDE : (k + 1) * WIDE] for k in range(block.shape[2] // WIDE)]


def fill_wide(tab, first, comps, blocks):
    per_comp = tab.shape[1] // comps
    for c in range(comps):
        pieces = [piece for block in blocks for piece in wide_pieces(block, c)]
        for k in range(0, len(pieces), 4):
            stack = jnp.concatenate(pieces[k : k + 4], 0)
            big = stack.astype(bf16)
            rows = pl.ds(c * per_comp + (first + k) * 4, 16)
            tab[0, rows, :] = big
            tab[1, rows, :] = (stack - big.astype(f32)).astype(bf16)


def wide_rows(near, quad, tile, base):
    first = 4 * quad + 2 * tile
    return [near[n : n + 1, pl.ds(base, LANES)] for n in (first, first + 1)]


def one_hot(rows):
    slot = lax.broadcasted_iota(i32, (WIDE, LANES), 0).astype(f32).astype(bf16)
    one, zero = jnp.ones((WIDE, LANES), bf16), jnp.zeros((WIDE, LANES), bf16)
    hits = []
    for r in rows:
        low = jnp.broadcast_to((r & (WIDE - 1)).astype(f32), (WIDE, LANES)).astype(bf16)
        hits.append(jnp.where(slot == low, one, zero))
    return jnp.concatenate(hits, 1)


def wide_find(tab, comps, weights, rows):
    found = jnp.dot(tab[0], weights, preferred_element_type=f32) + jnp.dot(
        tab[1], weights, preferred_element_type=f32
    )
    pairs = tab.shape[1] // comps // 8
    bits = max(pairs - 1, 0).bit_length()
    up = upper_half()
    highs = [row(r) >> 8 for r in rows]
    masks = [[(high & (2 << b)) != 0 for b in range(bits)] for high in highs]
    even = ((jnp.where(up, highs[1], highs[0]) & 1) == 1) == up

    def choose(c, side, bit, start):
        if bit < 0:
            top = (c * pairs + start) * 8
            return found[top : top + 8, side * LANES : (side + 1) * LANES]
        lower = choose(c, side, bit - 1, start)
        if start + (1 << bit) >= pairs:
            return lower
        return jnp.where(masks[side][bit], choose(c, side, bit - 1, start + (1 << bit)), lower)

    out = []
    for c in range(comps):
        a, b = choose(c, 0, bits - 1, 0), choose(c, 1, bits - 1, 0)
        crossed = pltpu.roll(jnp.where(up, a, b), 4, 0)
        out.append(jnp.where(even, jnp.where(up, b, a), crossed))
    return out


def fold(parts):
    sublane = lax.broadcasted_iota(i32, (8, LANES), 0)
    up, second = sublane >= 4, (sublane & 2) != 0
    outer = [
        jnp.where(up, b, a) + pltpu.roll(jnp.where(up, a, b), 4, 0)
        for a, b in ((parts[0], parts[2]), (parts[1], parts[3]))
    ]
    swapped = jnp.take_along_axis(jnp.where(second, outer[0], outer[1]), sublane ^ 2, axis=0)
    inner = jnp.where(second, outer[1], outer[0]) + swapped
    even = (sublane * 2) & 7
    both = jnp.take_along_axis(inner, even, axis=0) + jnp.take_along_axis(inner, even + 1, axis=0)
    return both[:4]


def forces(pos, ratio, lanes, there, params, quads):
    force = [[None] * 4 for _ in range(3)]
    for quad in range(quads):
        for half in range(2):
            other = [there[quad, half, c] for c in range(3)]
            charge, depth = params[quad, half, 0], params[quad, half, 1]
            for i in range(4):
                offset = [row(pos[c, i : i + 1, lanes]) - other[c] for c in range(3)]
                square = offset[0] * offset[0] + (offset[1] * offset[1] + (offset[2] * offset[2] + softening))
                root = lax.rsqrt(square)
                cube = root * root * root
                weight = cube * (row(ratio[i : i + 1, lanes]) * charge + depth * (cube - root))
                for c in range(3):
                    term = weight * offset[c]
                    force[c][i] = term if quad + half == 0 else force[c][i] + term
    return [fold(force[c]) for c in range(3)]


def kernel(
    partner_in, order_in, coupling_in, phase_in, charges_in, lj_in, fill_in, near_in, gs_in, out,
    partner, scale_order, coupling, phase, charges, lj, fill, near, gs, ratio, spot_even, spot_odd,
    from_low, from_high, par, par_first, par_last, par_low, par_high,
    pos_first, pos_last, pos_low, pos_high, pos, pos_next, vel,
    exact, packed_par, packed_pos, gathered, part, part_par, wide_par, wide_pos, hot, ready_sem, load_sem, send_sem, recv_sem,
):
    total, width = phase.shape[2], gs.shape[1] // 2
    own, ghost = total // LANES, width // LANES
    tiles = own + 2 * ghost
    quads = near.shape[0] // 4
    slim = quads - WIDE_QUADS
    level, levels = lax.axis_index("rep"), lax.axis_size("rep")
    place, places = lax.axis_index("space"), lax.axis_size("space")
    has_low, has_high = level > 0, level < levels - 1
    above, below = lax.rem(place + 1, places), lax.rem(place + places - 1, places)

    barrier = pltpu.get_barrier_semaphore()

    def greet(device):
        pl.semaphore_signal(barrier, inc=1, device_id=device, device_id_type=MESH)

    odd = lax.rem(place, 2) == 1

    @pl.when(jnp.logical_not(odd))
    def _():
        greet({"space": above})
        greet({"space": below})

    @pl.when(has_low)
    def _():
        greet({"rep": level - 1})

    @pl.when(has_high)
    def _():
        greet({"rep": level + 1})

    loads = [
        pltpu.make_async_copy(src, dst, load_sem.at[n])
        for n, (src, dst) in enumerate(
            [
                (phase_in, phase), (fill_in, fill), (charges_in, charges), (lj_in, lj), (gs_in, gs), (near_in, near),
                (partner_in, partner), (order_in, scale_order), (coupling_in, coupling),
            ]
        )
    ]
    for copy in loads:
        copy.start()

    def remote(src, dst, number, device):
        return pltpu.make_async_remote_copy(
            src_ref=src, dst_ref=dst, send_sem=send_sem.at[number], recv_sem=recv_sem.at[number],
            device_id=device, device_id_type=MESH,
        )

    def ring(first, last, low, high, number):
        return [remote(last, low, number, {"space": above}), remote(first, high, number + 1, {"space": below})]

    def each_group(start, stop, body):
        def step(group, carry):
            body(group, pl.multiple_of(group * LANES, LANES))
            return carry

        lax.fori_loop(start, stop, step, 0, unroll=2)

    pl.semaphore_wait(barrier, jnp.where(odd, 2, 0) + jnp.where(has_low, 1, 0) + jnp.where(has_high, 1, 0))

    @pl.when(odd)
    def _():
        for neighbour in (above, below):
            pl.semaphore_signal(ready_sem, inc=1, device_id={"space": neighbour}, device_id_type=MESH)

    loads[0].wait()

    halves = (pl.ds(0, 3), pl.ds(3, 3))
    rising = [remote(phase.at[h], from_low.at[h], n, {"rep": level + 1}) for n, h in enumerate(halves)]
    falling = [remote(phase.at[h], from_high.at[h], 2 + n, {"rep": level - 1}) for n, h in enumerate(halves)]

    def swap_start(n):
        @pl.when(has_high)
        def _():
            rising[n].start()

        @pl.when(has_low)
        def _():
            falling[n].start()

    def swap_arrived(n):
        @pl.when(has_low)
        def _():
            rising[n].wait_recv()

        @pl.when(has_high)
        def _():
            falling[n].wait_recv()

    swap_start(0)

    for copy in loads[1:5]:
        copy.wait()
    slot = lax.broadcasted_iota(i32, (4, total), 0)
    present = (slot < fill[...]).astype(f32)
    par[0] = charges[...] * present
    par[1] = lj[...] * present
    ratio[...] = charges[...] / lj[...]
    for c in range(2):
        fill_exact(exact.at[c], par[c])
    gather_ghosts(exact, 2, own, gs, par_first, par_last)
    par_tabs = [packed_par.at[0], packed_par.at[1]]
    pack_params(par_tabs, 0, par)
    fill_wide(wide_par, 0, 2, [par])

    def look_ahead(tabs, kept, group, base):
        for quad in range(slim):
            index = quad_index(near, quad, base)
            for n, word in enumerate(lookup(tabs, 0, own, index & (LANES - 1), index >> 7)):
                kept[group, quad, n] = word

    def params_ahead(group, base):
        look_ahead(par_tabs, part_par, group, base)
        for quad in range(slim, quads):
            for tile in range(2):
                hot[group, quad - slim, tile] = one_hot(wide_rows(near, quad, tile, base))

    for copy in loads[5:]:
        copy.wait()
    each_group(0, own, params_ahead)


    def find_rest(tabs, kept, group, quad, index):
        words = lookup(tabs, own, tiles - own, index & (LANES - 1), (index >> 7) - own)
        return [jnp.where(index < total, kept[group, quad, n], word) for n, word in enumerate(words)]

    moved = partner[level] - level

    def swapped(c, lanes):
        return jnp.where(
            moved == 0, phase[c, :, lanes],
            jnp.where(moved < 0, from_low[c, :, lanes], from_high[c, :, lanes]),
        )

    swap_arrived(0)
    for c in range(3):
        block = swapped(c, pl.ds(0, total))
        pos[c] = block
        fill_exact(exact.at[c], block)
    gather_ghosts(exact, 3, own, gs, pos_first.at[0], pos_last.at[0])
    pos_rings = [
        ring(pos_first.at[n], pos_last.at[n], pos_low.at[n], pos_high.at[n], 6 + 2 * n) for n in range(2)
    ]
    par_ring = ring(par_first, par_last, par_low, par_high, 4)

    @pl.when(jnp.logical_not(odd))
    def _():
        pl.semaphore_wait(ready_sem, 2)

    for copy in par_ring + pos_rings[0]:
        copy.start()
    swap_start(1)
    tabs = [packed_pos.at[n] for n in range(3)]
    top_own = largest([pos])
    pack_positions(tabs, 0, pos, top_own)
    fill_wide(wide_pos, 0, 3, [pos])
    unit_own = top_own * UNIT

    each_group(0, own, lambda group, base: look_ahead(tabs, part, group, base))

    for copy in par_ring:
        copy.wait_recv()
    pack_params(par_tabs, own, par_low)
    pack_params(par_tabs, own + ghost, par_high)
    wide_own = total // WIDE
    fill_wide(wide_par, wide_own, 2, [par_low, par_high])
    strength = coupling[scale_order[level]]

    def wide_params(group, base):
        for quad in range(slim, quads):
            for tile in range(2):
                rows = wide_rows(near, quad, tile, base)
                charge, depth = wide_find(wide_par, 2, hot[group, quad - slim, tile], rows)
                gathered[group, quad, tile, 0] = charge * strength
                gathered[group, quad, tile, 1] = depth

    def finish_params(group):
        base = pl.multiple_of(group * LANES, LANES)
        for quad in range(slim):
            words = find_rest(par_tabs, part_par, group, quad, quad_index(near, quad, base))
            for half, word in enumerate(words):
                gathered[group, quad, half, 0] = (word >> 16).astype(f32) * (strength * (1.0 / Q_STEPS))
                gathered[group, quad, half, 1] = (word & 65535).astype(f32) * (1.0 / E_STEPS)

    def ghosts_arrived(n):
        for copy in pos_rings[n]:
            copy.wait_recv()
        low, high = pos_low.at[n], pos_high.at[n]
        top = largest([low, high])
        pack_positions(tabs, own, low, top)
        pack_positions(tabs, own + ghost, high, top)
        fill_wide(wide_pos, wide_own, 3, [low, high])
        return top * UNIT

    def find(group, spot, unit_here, unit_there):
        base = pl.multiple_of(group * LANES, LANES)
        for quad in range(quads):
            if quad < slim:
                index = quad_index(near, quad, base)
                words = find_rest(tabs, part, group, quad, index)
                pair = unpack_positions(words, jnp.where(index < total, unit_here, unit_there))
            else:
                pair = [
                    wide_find(wide_pos, 3, hot[group, quad - slim, tile], wide_rows(near, quad, tile, base))
                    for tile in range(2)
                ]
            for half in range(2):
                for c in range(3):
                    spot[quad, half, c] = pair[half][c]

    def move_all(move, prepare):
        prepare(0, spot_even)

        def step(couple, carry):
            group = 2 * couple
            move(group, spot_even)
            prepare(group + 1, spot_odd)
            move(group + 1, spot_odd)
            prepare(jnp.minimum(group + 2, own - 1), spot_even)
            return carry

        lax.fori_loop(0, own // 2, step, 0)

    def force_on(where, group, spot):
        lanes = pl.ds(pl.multiple_of(group * LANES, LANES), LANES)
        depth = par[1, :, lanes]
        return lanes, [f * depth for f in forces(where, ratio, lanes, spot, gathered.at[group], quads)]

    swap_arrived(1)
    unit_ghost = ghosts_arrived(0)

    def first_step(group, spot):
        lanes, force = force_on(pos, group, spot)
        for c in range(3):
            v = swapped(3 + c, lanes) + time_step * force[c]
            vel[c, :, lanes] = v
            pos_next[c, :, lanes] = pos[c, :, lanes] + time_step * v

    def first_prepare(group, spot):
        finish_params(group)
        wide_params(group, pl.multiple_of(group * LANES, LANES))
        find(group, spot, unit_own, unit_ghost)

    move_all(first_step, first_prepare)

    for c in range(3):
        fill_exact(exact.at[c], pos_next[c])
    gather_ghosts(exact, 3, own, gs, pos_first.at[1], pos_last.at[1])
    for copy in pos_rings[1]:
        copy.start()
    top_own = largest([pos_next])
    pack_positions(tabs, 0, pos_next, top_own)
    fill_wide(wide_pos, 0, 3, [pos_next])
    unit_own_next = top_own * UNIT

    each_group(0, own, lambda group, base: look_ahead(tabs, part, group, base))
    unit_ghost_next = ghosts_arrived(1)

    def second_step(group, spot):
        lanes, force = force_on(pos_next, group, spot)
        for c in range(3):
            v = vel[c, :, lanes] + time_step * force[c]
            out[3 + c, :, lanes] = v
            out[c, :, lanes] = pos_next[c, :, lanes] + time_step * v

    move_all(second_step, lambda group, spot: find(group, spot, unit_own_next, unit_ghost_next))

    for copy in par_ring + pos_rings[0] + pos_rings[1]:
        copy.wait_send()
    for n in range(2):

        @pl.when(has_high)
        def _():
            rising[n].wait_send()

        @pl.when(has_low)
        def _():
            falling[n].wait_send()


def on_device(
    phase_space, charges, lj_depth, cluster_fill, neighbours, ghost_send, partner, scale_order, coupling
):
    phase = phase_space[0]
    rows, slots, total = phase.shape
    width = ghost_send.shape[1] // 2
    own = total // LANES
    tiles = own + 2 * (width // LANES)
    quads = neighbours.shape[1] // 4
    wides = tiles * LANES // WIDE
    out = pl.pallas_call(
        kernel,
        out_shape=pltpu.VMEM(phase.shape, f32),
        in_specs=[pl.BlockSpec(memory_space=pltpu.HBM)] * 9,
        out_specs=VMEM,
        scratch_shapes=[
            pltpu.SMEM(partner.shape, i32),
            pltpu.SMEM(scale_order.shape, i32),
            pltpu.SMEM(coupling.shape, f32),
            pltpu.VMEM((rows, slots, total), f32),
            pltpu.VMEM((slots, total), f32),
            pltpu.VMEM((slots, total), f32),
            pltpu.VMEM((1, total), i32),
            pltpu.VMEM((4 * quads, total), i32),
            pltpu.VMEM((1, 2 * width), i32),
            pltpu.VMEM((slots, total), f32),
            pltpu.VMEM((quads, 2, 3, 8, LANES), f32),
            pltpu.VMEM((quads, 2, 3, 8, LANES), f32),
            pltpu.VMEM((rows, slots, total), f32),
            pltpu.VMEM((rows, slots, total), f32),
            pltpu.VMEM((2, slots, total), f32),
        ]
        + [pltpu.VMEM((2, slots, width), f32)] * 4
        + [pltpu.VMEM((2, 3, slots, width), f32)] * 4
        + [pltpu.VMEM((3, slots, total), f32)] * 3
        + [
            pltpu.VMEM((3, own, 8, LANES), f32),
            pltpu.VMEM((2, tiles, 8, LANES), i32),
            pltpu.VMEM((3, tiles, 8, LANES), i32),
            pltpu.VMEM((own, quads, 2, 2, 8, LANES), f32),
            pltpu.VMEM((own, quads - WIDE_QUADS, 3, 8, LANES), i32),
            pltpu.VMEM((own, quads - WIDE_QUADS, 2, 8, LANES), i32),
            pltpu.VMEM((2, 2 * 4 * wides, WIDE), bf16),
            pltpu.VMEM((2, 3 * 4 * wides, WIDE), bf16),
            pltpu.VMEM((own, WIDE_QUADS, 2, WIDE, 2 * LANES), bf16),
            pltpu.SemaphoreType.REGULAR,
            pltpu.SemaphoreType.DMA((9,)),
            pltpu.SemaphoreType.DMA((10,)),
            pltpu.SemaphoreType.DMA((10,)),
        ],
        compiler_params=pltpu.CompilerParams(collective_id=0, has_side_effects=True),
    )(partner, scale_order, coupling, phase, charges[0], lj_depth[0], cluster_fill, neighbours[0], ghost_send)
    return out[None]


def solution(mesh):
    return jax.shard_map(
        on_device,
        mesh=mesh,
        in_specs=(
            P("rep", None, None, "space"),
            P("rep", None, "space"),
            P("rep", None, "space"),
            P("rep", "space"),
            P("rep", None, "space"),
            P("rep", "space"),
            P(),
            P(),
            P(),
        ),
        out_specs=P("rep", None, None, "space"),
        check_vma=False,
    )
```

```python
import jax
import jax.numpy as jnp
from jax import lax
from jax.experimental import pallas as pl
from jax.experimental.pallas import tpu as pltpu
from jax.sharding import PartitionSpec as P

STEPS = 2
LANES = 128

time_step = 0.2
softening = 0.5

VMEM = pl.BlockSpec(memory_space=pltpu.VMEM)
MESH = pl.DeviceIdType.MESH
f32 = jnp.float32
i32 = jnp.int32
bf16 = jnp.bfloat16

WIDE = 256
WIDE_QUADS = 1

POS = 32766.0
UNIT = 1.0 / (POS * 65536)
Q_STEPS = 8191.0
E_STEPS = 32767.0


def upper_half():
    return lax.broadcasted_iota(i32, (8, LANES), 0) >= 4


def row(values):
    return jnp.broadcast_to(values, (8, LANES))


def twice(tile):
    return jnp.concatenate([tile, tile], 0)


def lookup(tabs, first, count, low, high):
    bits = max(count - 1, 0).bit_length()
    masks = [(high & (1 << b)) != 0 for b in range(bits)]

    def find(tab, bit, start):
        if bit < 0:
            return jnp.take_along_axis(tab[first + start], low, axis=1)
        lower = find(tab, bit - 1, start)
        if start + (1 << bit) >= count:
            return lower
        return jnp.where(masks[bit], find(tab, bit - 1, start + (1 << bit)), lower)

    return [find(tab, bits - 1, 0) for tab in tabs]


def quad_index(near, quad, base):
    rows = [row(near[4 * quad + n : 4 * quad + n + 1, pl.ds(base, LANES)]) for n in range(4)]
    sublane = lax.broadcasted_iota(i32, (8, LANES), 0)
    return jnp.where(
        sublane < 4,
        jnp.where(sublane < 2, rows[0], rows[1]),
        jnp.where(sublane < 6, rows[2], rows[3]),
    )


def two_rows(first, second):
    odd = (lax.broadcasted_iota(i32, (8, LANES), 0) & 1) == 1
    return jnp.where(odd, row(second), row(first))


def low16(word):
    return (word << 16) >> 16


def fill_exact(tab, block):
    for k in range(block.shape[1] // LANES):
        tab[k] = twice(block[:, k * LANES : (k + 1) * LANES])


def gather_ghosts(tab, comps, own, gs, out_first, out_last):
    width = out_first.shape[2]
    up = upper_half()
    for g in range(width // LANES):
        index = jnp.where(
            up,
            row(gs[:, width + g * LANES : width + (g + 1) * LANES]),
            row(gs[:, g * LANES : (g + 1) * LANES]),
        )
        found = lookup([tab.at[c] for c in range(comps)], 0, own, index & (LANES - 1), index >> 7)
        for c in range(comps):
            out_first[c, :, g * LANES : (g + 1) * LANES] = found[c][:4]
            out_last[c, :, g * LANES : (g + 1) * LANES] = found[c][4:]


def pack_params(tabs, first, par):
    for k in range(par.shape[2] // LANES):
        cut = slice(k * LANES, (k + 1) * LANES)
        q = (par[0, :, cut] * Q_STEPS + 32768.5).astype(i32) - 32768
        e = (par[1, :, cut] * E_STEPS + 0.5).astype(i32)
        word = (q << 16) | e
        for half in range(2):
            tabs[half][first + k] = two_rows(word[2 * half : 2 * half + 1], word[2 * half + 1 : 2 * half + 2])


def largest(blocks):
    top = None
    for block in blocks:
        for c in range(3):
            here = jnp.max(jnp.abs(block[c]), axis=0, keepdims=True)
            here = jnp.max(here, axis=1, keepdims=True)
            top = here if top is None else jnp.maximum(top, here)
    return jnp.maximum(top, 1e-30)


def both_halves(high, low):
    low = ((low + 32768.5).astype(i32) - 32768) & 65535
    high = (high + 32768.5 - low.astype(f32) * (1.0 / 65536)).astype(i32) - 32768
    return (high << 16) | low


def pack_positions(tabs, first, pos, top):
    factor = POS / top
    for k in range(pos.shape[2] // LANES):
        cut = slice(k * LANES, (k + 1) * LANES)
        x, y, z = [pos[c, :, cut] * factor for c in range(3)]
        word = both_halves(x, y)
        depth = both_halves(z[0:2], z[2:4])
        tabs[0][first + k] = two_rows(word[0:1], word[1:2])
        tabs[1][first + k] = two_rows(word[2:3], word[3:4])
        tabs[2][first + k] = two_rows(depth[0:1], depth[1:2])


def unpack_positions(words, unit):
    third = (words[2], words[2] << 16)
    return [
        [v.astype(f32) * unit for v in (words[half], words[half] << 16, third[half])] for half in range(2)
    ]


def wide_pieces(block, c):
    return [block[c, :, k * WIDE : (k + 1) * WIDE] for k in range(block.shape[2] // WIDE)]


def fill_wide(tab, first, comps, blocks):
    per_comp = tab.shape[1] // comps
    for c in range(comps):
        pieces = [piece for block in blocks for piece in wide_pieces(block, c)]
        for k in range(0, len(pieces), 4):
            stack = jnp.concatenate(pieces[k : k + 4], 0)
            big = stack.astype(bf16)
            rows = pl.ds(c * per_comp + (first + k) * 4, 16)
            tab[0, rows, :] = big
            tab[1, rows, :] = (stack - big.astype(f32)).astype(bf16)


def wide_rows(near, quad, tile, base):
    first = 4 * quad + 2 * tile
    return [near[n : n + 1, pl.ds(base, LANES)] for n in (first, first + 1)]


def one_hot(rows):
    slot = lax.broadcasted_iota(i32, (WIDE, LANES), 0).astype(f32).astype(bf16)
    one, zero = jnp.ones((WIDE, LANES), bf16), jnp.zeros((WIDE, LANES), bf16)
    hits = []
    for r in rows:
        low = jnp.broadcast_to((r & (WIDE - 1)).astype(f32), (WIDE, LANES)).astype(bf16)
        hits.append(jnp.where(slot == low, one, zero))
    return jnp.concatenate(hits, 1)


def wide_find(tab, comps, weights, rows):
    found = jnp.dot(tab[0], weights, preferred_element_type=f32) + jnp.dot(
        tab[1], weights, preferred_element_type=f32
    )
    pairs = tab.shape[1] // comps // 8
    bits = max(pairs - 1, 0).bit_length()
    up = upper_half()
    highs = [row(r) >> 8 for r in rows]
    masks = [[(high & (2 << b)) != 0 for b in range(bits)] for high in highs]
    even = ((jnp.where(up, highs[1], highs[0]) & 1) == 1) == up

    def choose(c, side, bit, start):
        if bit < 0:
            top = (c * pairs + start) * 8
            return found[top : top + 8, side * LANES : (side + 1) * LANES]
        lower = choose(c, side, bit - 1, start)
        if start + (1 << bit) >= pairs:
            return lower
        return jnp.where(masks[side][bit], choose(c, side, bit - 1, start + (1 << bit)), lower)

    out = []
    for c in range(comps):
        a, b = choose(c, 0, bits - 1, 0), choose(c, 1, bits - 1, 0)
        crossed = pltpu.roll(jnp.where(up, a, b), 4, 0)
        out.append(jnp.where(even, jnp.where(up, b, a), crossed))
    return out


def fold(parts):
    sublane = lax.broadcasted_iota(i32, (8, LANES), 0)
    up, second = sublane >= 4, (sublane & 2) != 0
    outer = [
        jnp.where(up, b, a) + pltpu.roll(jnp.where(up, a, b), 4, 0)
        for a, b in ((parts[0], parts[2]), (parts[1], parts[3]))
    ]
    swapped = jnp.take_along_axis(jnp.where(second, outer[0], outer[1]), sublane ^ 2, axis=0)
    inner = jnp.where(second, outer[1], outer[0]) + swapped
    even = (sublane * 2) & 7
    both = jnp.take_along_axis(inner, even, axis=0) + jnp.take_along_axis(inner, even + 1, axis=0)
    return both[:4]


def forces(pos, ratio, lanes, there, params, quads):
    force = [[None] * 4 for _ in range(3)]
    for quad in range(quads):
        for half in range(2):
            other = [there[quad, half, c] for c in range(3)]
            charge, depth = params[quad, half, 0], params[quad, half, 1]
            for i in range(4):
                offset = [row(pos[c, i : i + 1, lanes]) - other[c] for c in range(3)]
                square = offset[0] * offset[0] + (offset[1] * offset[1] + (offset[2] * offset[2] + softening))
                root = lax.rsqrt(square)
                cube = root * root * root
                weight = cube * (row(ratio[i : i + 1, lanes]) * charge + depth * (cube - root))
                for c in range(3):
                    term = weight * offset[c]
                    force[c][i] = term if quad + half == 0 else force[c][i] + term
    return [fold(force[c]) for c in range(3)]


def kernel(
    partner_in, order_in, coupling_in, phase_in, charges_in, lj_in, fill_in, near_in, gs_in, out,
    partner, scale_order, coupling, phase, charges, lj, fill, near, gs, ratio, spot_even, spot_odd,
    from_low, from_high, par, par_first, par_last, par_low, par_high,
    pos_first, pos_last, pos_low, pos_high, pos, pos_next, vel,
    exact, packed_par, packed_pos, gathered, part, part_par, wide_par, wide_pos, hot, ready_sem, load_sem, send_sem, recv_sem,
):
    total, width = phase.shape[2], gs.shape[1] // 2
    own, ghost = total // LANES, width // LANES
    tiles = own + 2 * ghost
    early = own - own // 4
    quads = near.shape[0] // 4
    slim = quads - WIDE_QUADS
    level, levels = lax.axis_index("rep"), lax.axis_size("rep")
    place, places = lax.axis_index("space"), lax.axis_size("space")
    has_low, has_high = level > 0, level < levels - 1
    above, below = lax.rem(place + 1, places), lax.rem(place + places - 1, places)

    barrier = pltpu.get_barrier_semaphore()

    def greet(device):
        pl.semaphore_signal(barrier, inc=1, device_id=device, device_id_type=MESH)

    odd = lax.rem(place, 2) == 1

    @pl.when(jnp.logical_not(odd))
    def _():
        greet({"space": above})
        greet({"space": below})

    @pl.when(has_low)
    def _():
        greet({"rep": level - 1})

    @pl.when(has_high)
    def _():
        greet({"rep": level + 1})

    loads = [
        pltpu.make_async_copy(src, dst, load_sem.at[n])
        for n, (src, dst) in enumerate(
            [
                (phase_in, phase), (fill_in, fill), (charges_in, charges), (lj_in, lj), (gs_in, gs), (near_in, near),
                (partner_in, partner), (order_in, scale_order), (coupling_in, coupling),
            ]
        )
    ]
    for copy in loads:
        copy.start()

    def remote(src, dst, number, device):
        return pltpu.make_async_remote_copy(
            src_ref=src, dst_ref=dst, send_sem=send_sem.at[number], recv_sem=recv_sem.at[number],
            device_id=device, device_id_type=MESH,
        )

    def ring(first, last, low, high, number):
        return [remote(last, low, number, {"space": above}), remote(first, high, number + 1, {"space": below})]

    def each_group(start, stop, body):
        def step(group, carry):
            body(group, pl.multiple_of(group * LANES, LANES))
            return carry

        lax.fori_loop(start, stop, step, 0, unroll=4)

    pl.semaphore_wait(barrier, jnp.where(odd, 2, 0) + jnp.where(has_low, 1, 0) + jnp.where(has_high, 1, 0))

    @pl.when(odd)
    def _():
        for neighbour in (above, below):
            pl.semaphore_signal(ready_sem, inc=1, device_id={"space": neighbour}, device_id_type=MESH)

    loads[0].wait()

    halves = (pl.ds(0, 3), pl.ds(3, 3))
    rising = [remote(phase.at[h], from_low.at[h], n, {"rep": level + 1}) for n, h in enumerate(halves)]
    falling = [remote(phase.at[h], from_high.at[h], 2 + n, {"rep": level - 1}) for n, h in enumerate(halves)]

    def swap_start(n):
        @pl.when(has_high)
        def _():
            rising[n].start()

        @pl.when(has_low)
        def _():
            falling[n].start()

    def swap_arrived(n):
        @pl.when(has_low)
        def _():
            rising[n].wait_recv()

        @pl.when(has_high)
        def _():
            falling[n].wait_recv()

    swap_start(0)

    for copy in loads[1:5]:
        copy.wait()
    slot = lax.broadcasted_iota(i32, (4, total), 0)
    present = (slot < fill[...]).astype(f32)
    par[0] = charges[...] * present
    par[1] = lj[...] * present
    ratio[...] = charges[...] / lj[...]
    for c in range(2):
        fill_exact(exact.at[c], par[c])
    gather_ghosts(exact, 2, own, gs, par_first, par_last)
    par_tabs = [packed_par.at[0], packed_par.at[1]]
    pack_params(par_tabs, 0, par)
    fill_wide(wide_par, 0, 2, [par])

    def look_ahead(tabs, kept, group, base):
        for quad in range(slim):
            index = quad_index(near, quad, base)
            for n, word in enumerate(lookup(tabs, 0, own, index & (LANES - 1), index >> 7)):
                kept[group, quad, n] = word

    def params_ahead(group, base):
        look_ahead(par_tabs, part_par, group, base)
        for quad in range(slim, quads):
            for tile in range(2):
                hot[group, quad - slim, tile] = one_hot(wide_rows(near, quad, tile, base))

    for copy in loads[5:]:
        copy.wait()
    each_group(0, early, params_ahead)


    def find_rest(tabs, kept, group, quad, index):
        words = lookup(tabs, own, tiles - own, index & (LANES - 1), (index >> 7) - own)
        return [jnp.where(index < total, kept[group, quad, n], word) for n, word in enumerate(words)]

    moved = partner[level] - level

    def swapped(c, lanes):
        return jnp.where(
            moved == 0, phase[c, :, lanes],
            jnp.where(moved < 0, from_low[c, :, lanes], from_high[c, :, lanes]),
        )

    swap_arrived(0)
    for c in range(3):
        block = swapped(c, pl.ds(0, total))
        pos[c] = block
        fill_exact(exact.at[c], block)
    gather_ghosts(exact, 3, own, gs, pos_first.at[0], pos_last.at[0])
    pos_rings = [
        ring(pos_first.at[n], pos_last.at[n], pos_low.at[n], pos_high.at[n], 6 + 2 * n) for n in range(2)
    ]
    par_ring = ring(par_first, par_last, par_low, par_high, 4)

    @pl.when(jnp.logical_not(odd))
    def _():
        pl.semaphore_wait(ready_sem, 2)

    for copy in par_ring + pos_rings[0]:
        copy.start()
    swap_start(1)
    tabs = [packed_pos.at[n] for n in range(3)]
    top_own = largest([pos])
    pack_positions(tabs, 0, pos, top_own)
    fill_wide(wide_pos, 0, 3, [pos])
    unit_own = top_own * UNIT

    each_group(0, own, lambda group, base: look_ahead(tabs, part, group, base))
    each_group(early, own, params_ahead)

    for copy in par_ring:
        copy.wait_recv()
    pack_params(par_tabs, own, par_low)
    pack_params(par_tabs, own + ghost, par_high)
    wide_own = total // WIDE
    fill_wide(wide_par, wide_own, 2, [par_low, par_high])
    strength = coupling[scale_order[level]]

    def wide_params(group, base):
        for quad in range(slim, quads):
            for tile in range(2):
                rows = wide_rows(near, quad, tile, base)
                charge, depth = wide_find(wide_par, 2, hot[group, quad - slim, tile], rows)
                gathered[group, quad, tile, 0] = charge * strength
                gathered[group, quad, tile, 1] = depth

    def finish_params(group):
        base = pl.multiple_of(group * LANES, LANES)
        for quad in range(slim):
            words = find_rest(par_tabs, part_par, group, quad, quad_index(near, quad, base))
            for half, word in enumerate(words):
                gathered[group, quad, half, 0] = (word >> 16).astype(f32) * (strength * (1.0 / Q_STEPS))
                gathered[group, quad, half, 1] = (word & 65535).astype(f32) * (1.0 / E_STEPS)

    def ghosts_arrived(n):
        for copy in pos_rings[n]:
            copy.wait_recv()
        low, high = pos_low.at[n], pos_high.at[n]
        top = largest([low, high])
        pack_positions(tabs, own, low, top)
        pack_positions(tabs, own + ghost, high, top)
        fill_wide(wide_pos, wide_own, 3, [low, high])
        return top * UNIT

    def find(group, spot, unit_here, unit_there):
        base = pl.multiple_of(group * LANES, LANES)
        for quad in range(quads):
            if quad < slim:
                index = quad_index(near, quad, base)
                words = find_rest(tabs, part, group, quad, index)
                pair = unpack_positions(words, jnp.where(index < total, unit_here, unit_there))
            else:
                pair = [
                    wide_find(wide_pos, 3, hot[group, quad - slim, tile], wide_rows(near, quad, tile, base))
                    for tile in range(2)
                ]
            for half in range(2):
                for c in range(3):
                    spot[quad, half, c] = pair[half][c]

    def move_all(move, prepare):
        prepare(0, spot_even)

        def step(turn, carry):
            for n in range(8):
                here, there = (spot_even, spot_odd) if n % 2 == 0 else (spot_odd, spot_even)
                group = 8 * turn + n
                move(group, here)
                prepare(group + 1 if n < 7 else jnp.minimum(group + 1, own - 1), there)
            return carry

        lax.fori_loop(0, own // 8, step, 0)

    def force_on(where, group, spot):
        lanes = pl.ds(pl.multiple_of(group * LANES, LANES), LANES)
        depth = par[1, :, lanes]
        return lanes, [f * depth for f in forces(where, ratio, lanes, spot, gathered.at[group], quads)]

    swap_arrived(1)
    unit_ghost = ghosts_arrived(0)

    def first_step(group, spot):
        lanes, force = force_on(pos, group, spot)
        for c in range(3):
            v = swapped(3 + c, lanes) + time_step * force[c]
            vel[c, :, lanes] = v
            pos_next[c, :, lanes] = pos[c, :, lanes] + time_step * v

    def first_prepare(group, spot):
        finish_params(group)
        wide_params(group, pl.multiple_of(group * LANES, LANES))
        find(group, spot, unit_own, unit_ghost)

    move_all(first_step, first_prepare)

    for c in range(3):
        fill_exact(exact.at[c], pos_next[c])
    gather_ghosts(exact, 3, own, gs, pos_first.at[1], pos_last.at[1])
    for copy in pos_rings[1]:
        copy.start()
    top_own = largest([pos_next])
    pack_positions(tabs, 0, pos_next, top_own)
    fill_wide(wide_pos, 0, 3, [pos_next])
    unit_own_next = top_own * UNIT

    each_group(0, own, lambda group, base: look_ahead(tabs, part, group, base))
    unit_ghost_next = ghosts_arrived(1)

    def second_step(group, spot):
        lanes, force = force_on(pos_next, group, spot)
        for c in range(3):
            v = vel[c, :, lanes] + time_step * force[c]
            out[3 + c, :, lanes] = v
            out[c, :, lanes] = pos_next[c, :, lanes] + time_step * v

    move_all(second_step, lambda group, spot: find(group, spot, unit_own_next, unit_ghost_next))

    for copy in par_ring + pos_rings[0] + pos_rings[1]:
        copy.wait_send()
    for n in range(2):

        @pl.when(has_high)
        def _():
            rising[n].wait_send()

        @pl.when(has_low)
        def _():
            falling[n].wait_send()


def on_device(
    phase_space, charges, lj_depth, cluster_fill, neighbours, ghost_send, partner, scale_order, coupling
):
    phase = phase_space[0]
    rows, slots, total = phase.shape
    width = ghost_send.shape[1] // 2
    own = total // LANES
    tiles = own + 2 * (width // LANES)
    quads = neighbours.shape[1] // 4
    wides = tiles * LANES // WIDE
    out = pl.pallas_call(
        kernel,
        out_shape=pltpu.VMEM(phase.shape, f32),
        in_specs=[pl.BlockSpec(memory_space=pltpu.HBM)] * 9,
        out_specs=VMEM,
        scratch_shapes=[
            pltpu.SMEM(partner.shape, i32),
            pltpu.SMEM(scale_order.shape, i32),
            pltpu.SMEM(coupling.shape, f32),
            pltpu.VMEM((rows, slots, total), f32),
            pltpu.VMEM((slots, total), f32),
            pltpu.VMEM((slots, total), f32),
            pltpu.VMEM((1, total), i32),
            pltpu.VMEM((4 * quads, total), i32),
            pltpu.VMEM((1, 2 * width), i32),
            pltpu.VMEM((slots, total), f32),
            pltpu.VMEM((quads, 2, 3, 8, LANES), f32),
            pltpu.VMEM((quads, 2, 3, 8, LANES), f32),
            pltpu.VMEM((rows, slots, total), f32),
            pltpu.VMEM((rows, slots, total), f32),
            pltpu.VMEM((2, slots, total), f32),
        ]
        + [pltpu.VMEM((2, slots, width), f32)] * 4
        + [pltpu.VMEM((2, 3, slots, width), f32)] * 4
        + [pltpu.VMEM((3, slots, total), f32)] * 3
        + [
            pltpu.VMEM((3, own, 8, LANES), f32),
            pltpu.VMEM((2, tiles, 8, LANES), i32),
            pltpu.VMEM((3, tiles, 8, LANES), i32),
            pltpu.VMEM((own, quads, 2, 2, 8, LANES), f32),
            pltpu.VMEM((own, quads - WIDE_QUADS, 3, 8, LANES), i32),
            pltpu.VMEM((own, quads - WIDE_QUADS, 2, 8, LANES), i32),
            pltpu.VMEM((2, 2 * 4 * wides, WIDE), bf16),
            pltpu.VMEM((2, 3 * 4 * wides, WIDE), bf16),
            pltpu.VMEM((own, WIDE_QUADS, 2, WIDE, 2 * LANES), bf16),
            pltpu.SemaphoreType.REGULAR,
            pltpu.SemaphoreType.DMA((9,)),
            pltpu.SemaphoreType.DMA((10,)),
            pltpu.SemaphoreType.DMA((10,)),
        ],
        compiler_params=pltpu.CompilerParams(collective_id=0, has_side_effects=True),
    )(partner, scale_order, coupling, phase, charges[0], lj_depth[0], cluster_fill, neighbours[0], ghost_send)
    return out[None]


def solution(mesh):
    return jax.shard_map(
        on_device,
        mesh=mesh,
        in_specs=(
            P("rep", None, None, "space"),
            P("rep", None, "space"),
            P("rep", None, "space"),
            P("rep", "space"),
            P("rep", None, "space"),
            P("rep", "space"),
            P(),
            P(),
            P(),
        ),
        out_specs=P("rep", None, None, "space"),
        check_vma=False,
    )
```

```python
import jax
import jax.numpy as jnp
from jax import lax
from jax.experimental import pallas as pl
from jax.experimental.pallas import tpu as pltpu
from jax.sharding import PartitionSpec as P

STEPS = 2
LANES = 128

time_step = 0.2
softening = 0.5

VMEM = pl.BlockSpec(memory_space=pltpu.VMEM)
MESH = pl.DeviceIdType.MESH
f32 = jnp.float32
i32 = jnp.int32
bf16 = jnp.bfloat16

WIDE = 256
WIDE_QUADS = 1

POS = 32766.0
UNIT = 1.0 / (POS * 65536)
Q_STEPS = 8191.0
E_STEPS = 32767.0


def upper_half():
    return lax.broadcasted_iota(i32, (8, LANES), 0) >= 4


def row(values):
    return jnp.broadcast_to(values, (8, LANES))


def twice(tile):
    return jnp.concatenate([tile, tile], 0)


def lookup(tabs, first, count, low, high):
    bits = max(count - 1, 0).bit_length()
    masks = [(high & (1 << b)) != 0 for b in range(bits)]

    def find(tab, bit, start):
        if bit < 0:
            return jnp.take_along_axis(tab[first + start], low, axis=1)
        lower = find(tab, bit - 1, start)
        if start + (1 << bit) >= count:
            return lower
        return jnp.where(masks[bit], find(tab, bit - 1, start + (1 << bit)), lower)

    return [find(tab, bits - 1, 0) for tab in tabs]


def quad_index(near, quad, base):
    rows = [row(near[4 * quad + n : 4 * quad + n + 1, pl.ds(base, LANES)]) for n in range(4)]
    sublane = lax.broadcasted_iota(i32, (8, LANES), 0)
    return jnp.where(
        sublane < 4,
        jnp.where(sublane < 2, rows[0], rows[1]),
        jnp.where(sublane < 6, rows[2], rows[3]),
    )


def two_rows(first, second):
    odd = (lax.broadcasted_iota(i32, (8, LANES), 0) & 1) == 1
    return jnp.where(odd, row(second), row(first))


def low16(word):
    return (word << 16) >> 16


def fill_exact(tab, block):
    for k in range(block.shape[1] // LANES):
        tab[k] = twice(block[:, k * LANES : (k + 1) * LANES])


def gather_ghosts(tab, comps, own, gs, out_first, out_last):
    width = out_first.shape[2]
    up = upper_half()
    for g in range(width // LANES):
        index = jnp.where(
            up,
            row(gs[:, width + g * LANES : width + (g + 1) * LANES]),
            row(gs[:, g * LANES : (g + 1) * LANES]),
        )
        found = lookup([tab.at[c] for c in range(comps)], 0, own, index & (LANES - 1), index >> 7)
        for c in range(comps):
            out_first[c, :, g * LANES : (g + 1) * LANES] = found[c][:4]
            out_last[c, :, g * LANES : (g + 1) * LANES] = found[c][4:]


def pack_params(tabs, first, par):
    for k in range(par.shape[2] // LANES):
        cut = slice(k * LANES, (k + 1) * LANES)
        q = (par[0, :, cut] * Q_STEPS + 32768.5).astype(i32) - 32768
        e = (par[1, :, cut] * E_STEPS + 0.5).astype(i32)
        word = (q << 16) | e
        for half in range(2):
            tabs[half][first + k] = two_rows(word[2 * half : 2 * half + 1], word[2 * half + 1 : 2 * half + 2])


def largest(blocks):
    top = None
    for block in blocks:
        for c in range(3):
            here = jnp.max(jnp.abs(block[c]), axis=0, keepdims=True)
            here = jnp.max(here, axis=1, keepdims=True)
            top = here if top is None else jnp.maximum(top, here)
    return jnp.maximum(top, 1e-30)


def both_halves(high, low):
    low = ((low + 32768.5).astype(i32) - 32768) & 65535
    high = (high + 32768.5 - low.astype(f32) * (1.0 / 65536)).astype(i32) - 32768
    return (high << 16) | low


def pack_positions(tabs, first, pos, top):
    factor = POS / top
    for k in range(pos.shape[2] // LANES):
        cut = slice(k * LANES, (k + 1) * LANES)
        x, y, z = [pos[c, :, cut] * factor for c in range(3)]
        word = both_halves(x, y)
        depth = both_halves(z[0:2], z[2:4])
        tabs[0][first + k] = two_rows(word[0:1], word[1:2])
        tabs[1][first + k] = two_rows(word[2:3], word[3:4])
        tabs[2][first + k] = two_rows(depth[0:1], depth[1:2])


def unpack_positions(words, unit):
    third = (words[2], words[2] << 16)
    return [
        [v.astype(f32) * unit for v in (words[half], words[half] << 16, third[half])] for half in range(2)
    ]


def wide_pieces(block, c):
    return [block[c, :, k * WIDE : (k + 1) * WIDE] for k in range(block.shape[2] // WIDE)]


def fill_wide(tab, first, comps, blocks):
    per_comp = tab.shape[1] // comps
    for c in range(comps):
        pieces = [piece for block in blocks for piece in wide_pieces(block, c)]
        for k in range(0, len(pieces), 4):
            stack = jnp.concatenate(pieces[k : k + 4], 0)
            big = stack.astype(bf16)
            rows = pl.ds(c * per_comp + (first + k) * 4, 16)
            tab[0, rows, :] = big
            tab[1, rows, :] = (stack - big.astype(f32)).astype(bf16)


def wide_rows(near, quad, tile, base):
    first = 4 * quad + 2 * tile
    return [near[n : n + 1, pl.ds(base, LANES)] for n in (first, first + 1)]


def one_hot(rows):
    slot = lax.broadcasted_iota(i32, (WIDE, LANES), 0).astype(f32).astype(bf16)
    one, zero = jnp.ones((WIDE, LANES), bf16), jnp.zeros((WIDE, LANES), bf16)
    hits = []
    for r in rows:
        low = jnp.broadcast_to((r & (WIDE - 1)).astype(f32), (WIDE, LANES)).astype(bf16)
        hits.append(jnp.where(slot == low, one, zero))
    return jnp.concatenate(hits, 1)


def wide_find(tab, comps, weights, rows):
    found = jnp.dot(tab[0], weights, preferred_element_type=f32) + jnp.dot(
        tab[1], weights, preferred_element_type=f32
    )
    pairs = tab.shape[1] // comps // 8
    bits = max(pairs - 1, 0).bit_length()
    up = upper_half()
    highs = [row(r) >> 8 for r in rows]
    masks = [[(high & (2 << b)) != 0 for b in range(bits)] for high in highs]
    even = ((jnp.where(up, highs[1], highs[0]) & 1) == 1) == up

    def choose(c, side, bit, start):
        if bit < 0:
            top = (c * pairs + start) * 8
            return found[top : top + 8, side * LANES : (side + 1) * LANES]
        lower = choose(c, side, bit - 1, start)
        if start + (1 << bit) >= pairs:
            return lower
        return jnp.where(masks[side][bit], choose(c, side, bit - 1, start + (1 << bit)), lower)

    out = []
    for c in range(comps):
        a, b = choose(c, 0, bits - 1, 0), choose(c, 1, bits - 1, 0)
        crossed = pltpu.roll(jnp.where(up, a, b), 4, 0)
        out.append(jnp.where(even, jnp.where(up, b, a), crossed))
    return out


def fold(parts):
    sublane = lax.broadcasted_iota(i32, (8, LANES), 0)
    up, second = sublane >= 4, (sublane & 2) != 0
    outer = [
        jnp.where(up, b, a) + pltpu.roll(jnp.where(up, a, b), 4, 0)
        for a, b in ((parts[0], parts[2]), (parts[1], parts[3]))
    ]
    swapped = jnp.take_along_axis(jnp.where(second, outer[0], outer[1]), sublane ^ 2, axis=0)
    inner = jnp.where(second, outer[1], outer[0]) + swapped
    even = (sublane * 2) & 7
    both = jnp.take_along_axis(inner, even, axis=0) + jnp.take_along_axis(inner, even + 1, axis=0)
    return both[:4]


def forces(pos, ratio, lanes, there, params, quads):
    force = [[None] * 4 for _ in range(3)]
    for quad in range(quads):
        for half in range(2):
            other = [there[quad, half, c] for c in range(3)]
            charge, depth = params[quad, half, 0], params[quad, half, 1]
            for i in range(4):
                offset = [row(pos[c, i : i + 1, lanes]) - other[c] for c in range(3)]
                square = offset[0] * offset[0] + (offset[1] * offset[1] + (offset[2] * offset[2] + softening))
                root = lax.rsqrt(square)
                cube = root * root * root
                weight = cube * (row(ratio[i : i + 1, lanes]) * charge + depth * (cube - root))
                for c in range(3):
                    term = weight * offset[c]
                    force[c][i] = term if quad + half == 0 else force[c][i] + term
    return [fold(force[c]) for c in range(3)]


def kernel(
    partner_in, order_in, coupling_in, phase_in, charges_in, lj_in, fill_in, near_in, gs_in, out,
    partner, scale_order, coupling, phase, charges, lj, fill, near, gs, ratio, spot_even, spot_odd,
    from_low, from_high, par, par_first, par_last, par_low, par_high,
    pos_first, pos_last, pos_low, pos_high, pos, pos_next, vel,
    exact, packed_par, packed_pos, gathered, part, part_par, wide_par, wide_pos, hot, ready_sem, load_sem, send_sem, recv_sem,
):
    total, width = phase.shape[2], gs.shape[1] // 2
    own, ghost = total // LANES, width // LANES
    tiles = own + 2 * ghost
    early = own - own // 4
    quads = near.shape[0] // 4
    slim = quads - WIDE_QUADS
    level, levels = lax.axis_index("rep"), lax.axis_size("rep")
    place, places = lax.axis_index("space"), lax.axis_size("space")
    has_low, has_high = level > 0, level < levels - 1
    above, below = lax.rem(place + 1, places), lax.rem(place + places - 1, places)

    barrier = pltpu.get_barrier_semaphore()

    def greet(device):
        pl.semaphore_signal(barrier, inc=1, device_id=device, device_id_type=MESH)

    odd = lax.rem(place, 2) == 1

    @pl.when(jnp.logical_not(odd))
    def _():
        greet({"space": above})
        greet({"space": below})

    @pl.when(has_low)
    def _():
        greet({"rep": level - 1})

    @pl.when(has_high)
    def _():
        greet({"rep": level + 1})

    loads = [
        pltpu.make_async_copy(src, dst, load_sem.at[n])
        for n, (src, dst) in enumerate(
            [
                (phase_in, phase), (fill_in, fill), (charges_in, charges), (lj_in, lj), (gs_in, gs), (near_in, near),
                (partner_in, partner), (order_in, scale_order), (coupling_in, coupling),
            ]
        )
    ]
    for copy in loads:
        copy.start()

    def remote(src, dst, number, device):
        return pltpu.make_async_remote_copy(
            src_ref=src, dst_ref=dst, send_sem=send_sem.at[number], recv_sem=recv_sem.at[number],
            device_id=device, device_id_type=MESH,
        )

    def ring(first, last, low, high, number):
        return [remote(last, low, number, {"space": above}), remote(first, high, number + 1, {"space": below})]

    def each_group(start, stop, body):
        def step(group, carry):
            body(group, pl.multiple_of(group * LANES, LANES))
            return carry

        lax.fori_loop(start, stop, step, 0, unroll=4)

    pl.semaphore_wait(barrier, jnp.where(odd, 2, 0) + jnp.where(has_low, 1, 0) + jnp.where(has_high, 1, 0))

    @pl.when(odd)
    def _():
        for neighbour in (above, below):
            pl.semaphore_signal(ready_sem, inc=1, device_id={"space": neighbour}, device_id_type=MESH)

    halves = (pl.ds(0, 3), pl.ds(3, 3))
    rising = [remote(phase_in.at[h], from_low.at[h], n, {"rep": level + 1}) for n, h in enumerate(halves)]
    falling = [remote(phase_in.at[h], from_high.at[h], 2 + n, {"rep": level - 1}) for n, h in enumerate(halves)]

    def swap_start(n):
        @pl.when(has_high)
        def _():
            rising[n].start()

        @pl.when(has_low)
        def _():
            falling[n].start()

    def swap_arrived(n):
        @pl.when(has_low)
        def _():
            rising[n].wait_recv()

        @pl.when(has_high)
        def _():
            falling[n].wait_recv()

    swap_start(0)

    for copy in loads[1:5]:
        copy.wait()
    slot = lax.broadcasted_iota(i32, (4, total), 0)
    present = (slot < fill[...]).astype(f32)
    par[0] = charges[...] * present
    par[1] = lj[...] * present
    ratio[...] = charges[...] / lj[...]
    for c in range(2):
        fill_exact(exact.at[c], par[c])
    gather_ghosts(exact, 2, own, gs, par_first, par_last)
    par_tabs = [packed_par.at[0], packed_par.at[1]]
    pack_params(par_tabs, 0, par)
    fill_wide(wide_par, 0, 2, [par])

    def look_ahead(tabs, kept, group, base):
        for quad in range(slim):
            index = quad_index(near, quad, base)
            for n, word in enumerate(lookup(tabs, 0, own, index & (LANES - 1), index >> 7)):
                kept[group, quad, n] = word

    def params_ahead(group, base):
        look_ahead(par_tabs, part_par, group, base)
        for quad in range(slim, quads):
            for tile in range(2):
                hot[group, quad - slim, tile] = one_hot(wide_rows(near, quad, tile, base))

    for copy in loads[:1] + loads[5:]:
        copy.wait()
    each_group(0, early, params_ahead)


    def find_rest(tabs, kept, group, quad, index):
        words = lookup(tabs, own, tiles - own, index & (LANES - 1), (index >> 7) - own)
        return [jnp.where(index < total, kept[group, quad, n], word) for n, word in enumerate(words)]

    moved = partner[level] - level

    def swapped(c, lanes):
        return jnp.where(
            moved == 0, phase[c, :, lanes],
            jnp.where(moved < 0, from_low[c, :, lanes], from_high[c, :, lanes]),
        )

    swap_arrived(0)
    for c in range(3):
        block = swapped(c, pl.ds(0, total))
        pos[c] = block
        fill_exact(exact.at[c], block)
    gather_ghosts(exact, 3, own, gs, pos_first.at[0], pos_last.at[0])
    pos_rings = [
        ring(pos_first.at[n], pos_last.at[n], pos_low.at[n], pos_high.at[n], 6 + 2 * n) for n in range(2)
    ]
    par_ring = ring(par_first, par_last, par_low, par_high, 4)

    @pl.when(jnp.logical_not(odd))
    def _():
        pl.semaphore_wait(ready_sem, 2)

    for copy in par_ring + pos_rings[0]:
        copy.start()
    swap_start(1)
    tabs = [packed_pos.at[n] for n in range(3)]
    top_own = largest([pos])
    pack_positions(tabs, 0, pos, top_own)
    fill_wide(wide_pos, 0, 3, [pos])
    unit_own = top_own * UNIT

    each_group(0, own, lambda group, base: look_ahead(tabs, part, group, base))
    each_group(early, own, params_ahead)

    for copy in par_ring:
        copy.wait_recv()
    pack_params(par_tabs, own, par_low)
    pack_params(par_tabs, own + ghost, par_high)
    wide_own = total // WIDE
    fill_wide(wide_par, wide_own, 2, [par_low, par_high])
    strength = coupling[scale_order[level]]

    def wide_params(group, base):
        for quad in range(slim, quads):
            for tile in range(2):
                rows = wide_rows(near, quad, tile, base)
                charge, depth = wide_find(wide_par, 2, hot[group, quad - slim, tile], rows)
                gathered[group, quad, tile, 0] = charge * strength
                gathered[group, quad, tile, 1] = depth

    def finish_params(group):
        base = pl.multiple_of(group * LANES, LANES)
        for quad in range(slim):
            words = find_rest(par_tabs, part_par, group, quad, quad_index(near, quad, base))
            for half, word in enumerate(words):
                gathered[group, quad, half, 0] = (word >> 16).astype(f32) * (strength * (1.0 / Q_STEPS))
                gathered[group, quad, half, 1] = (word & 65535).astype(f32) * (1.0 / E_STEPS)

    def ghosts_arrived(n):
        for copy in pos_rings[n]:
            copy.wait_recv()
        low, high = pos_low.at[n], pos_high.at[n]
        top = largest([low, high])
        pack_positions(tabs, own, low, top)
        pack_positions(tabs, own + ghost, high, top)
        fill_wide(wide_pos, wide_own, 3, [low, high])
        return top * UNIT

    def find(group, spot, unit_here, unit_there):
        base = pl.multiple_of(group * LANES, LANES)
        for quad in range(quads):
            if quad < slim:
                index = quad_index(near, quad, base)
                words = find_rest(tabs, part, group, quad, index)
                pair = unpack_positions(words, jnp.where(index < total, unit_here, unit_there))
            else:
                pair = [
                    wide_find(wide_pos, 3, hot[group, quad - slim, tile], wide_rows(near, quad, tile, base))
                    for tile in range(2)
                ]
            for half in range(2):
                for c in range(3):
                    spot[quad, half, c] = pair[half][c]

    def move_all(move, prepare):
        prepare(0, spot_even)
        for group in range(own):
            here, there = (spot_even, spot_odd) if group % 2 == 0 else (spot_odd, spot_even)
            move(group, here)
            if group + 1 < own:
                prepare(group + 1, there)

    def force_on(where, group, spot):
        lanes = pl.ds(pl.multiple_of(group * LANES, LANES), LANES)
        depth = par[1, :, lanes]
        return lanes, [f * depth for f in forces(where, ratio, lanes, spot, gathered.at[group], quads)]

    swap_arrived(1)
    unit_ghost = ghosts_arrived(0)

    def first_step(group, spot):
        lanes, force = force_on(pos, group, spot)
        for c in range(3):
            v = swapped(3 + c, lanes) + time_step * force[c]
            vel[c, :, lanes] = v
            pos_next[c, :, lanes] = pos[c, :, lanes] + time_step * v

    def first_prepare(group, spot):
        finish_params(group)
        wide_params(group, pl.multiple_of(group * LANES, LANES))
        find(group, spot, unit_own, unit_ghost)

    move_all(first_step, first_prepare)

    for c in range(3):
        fill_exact(exact.at[c], pos_next[c])
    gather_ghosts(exact, 3, own, gs, pos_first.at[1], pos_last.at[1])
    for copy in pos_rings[1]:
        copy.start()
    top_own = largest([pos_next])
    pack_positions(tabs, 0, pos_next, top_own)
    fill_wide(wide_pos, 0, 3, [pos_next])
    unit_own_next = top_own * UNIT

    each_group(0, own, lambda group, base: look_ahead(tabs, part, group, base))
    unit_ghost_next = ghosts_arrived(1)

    def second_step(group, spot):
        lanes, force = force_on(pos_next, group, spot)
        for c in range(3):
            v = vel[c, :, lanes] + time_step * force[c]
            out[3 + c, :, lanes] = v
            out[c, :, lanes] = pos_next[c, :, lanes] + time_step * v

    move_all(second_step, lambda group, spot: find(group, spot, unit_own_next, unit_ghost_next))

    for copy in par_ring + pos_rings[0] + pos_rings[1]:
        copy.wait_send()
    for n in range(2):

        @pl.when(has_high)
        def _():
            rising[n].wait_send()

        @pl.when(has_low)
        def _():
            falling[n].wait_send()


def on_device(
    phase_space, charges, lj_depth, cluster_fill, neighbours, ghost_send, partner, scale_order, coupling
):
    phase = phase_space[0]
    rows, slots, total = phase.shape
    width = ghost_send.shape[1] // 2
    own = total // LANES
    tiles = own + 2 * (width // LANES)
    quads = neighbours.shape[1] // 4
    wides = tiles * LANES // WIDE
    out = pl.pallas_call(
        kernel,
        out_shape=pltpu.VMEM(phase.shape, f32),
        in_specs=[pl.BlockSpec(memory_space=pltpu.HBM)] * 9,
        out_specs=VMEM,
        scratch_shapes=[
            pltpu.SMEM(partner.shape, i32),
            pltpu.SMEM(scale_order.shape, i32),
            pltpu.SMEM(coupling.shape, f32),
            pltpu.VMEM((rows, slots, total), f32),
            pltpu.VMEM((slots, total), f32),
            pltpu.VMEM((slots, total), f32),
            pltpu.VMEM((1, total), i32),
            pltpu.VMEM((4 * quads, total), i32),
            pltpu.VMEM((1, 2 * width), i32),
            pltpu.VMEM((slots, total), f32),
            pltpu.VMEM((quads, 2, 3, 8, LANES), f32),
            pltpu.VMEM((quads, 2, 3, 8, LANES), f32),
            pltpu.VMEM((rows, slots, total), f32),
            pltpu.VMEM((rows, slots, total), f32),
            pltpu.VMEM((2, slots, total), f32),
        ]
        + [pltpu.VMEM((2, slots, width), f32)] * 4
        + [pltpu.VMEM((2, 3, slots, width), f32)] * 4
        + [pltpu.VMEM((3, slots, total), f32)] * 3
        + [
            pltpu.VMEM((3, own, 8, LANES), f32),
            pltpu.VMEM((2, tiles, 8, LANES), i32),
            pltpu.VMEM((3, tiles, 8, LANES), i32),
            pltpu.VMEM((own, quads, 2, 2, 8, LANES), f32),
            pltpu.VMEM((own, quads - WIDE_QUADS, 3, 8, LANES), i32),
            pltpu.VMEM((own, quads - WIDE_QUADS, 2, 8, LANES), i32),
            pltpu.VMEM((2, 2 * 4 * wides, WIDE), bf16),
            pltpu.VMEM((2, 3 * 4 * wides, WIDE), bf16),
            pltpu.VMEM((own, WIDE_QUADS, 2, WIDE, 2 * LANES), bf16),
            pltpu.SemaphoreType.REGULAR,
            pltpu.SemaphoreType.DMA((9,)),
            pltpu.SemaphoreType.DMA((10,)),
            pltpu.SemaphoreType.DMA((10,)),
        ],
        compiler_params=pltpu.CompilerParams(collective_id=0, has_side_effects=True),
    )(partner, scale_order, coupling, phase, charges[0], lj_depth[0], cluster_fill, neighbours[0], ghost_send)
    return out[None]


def solution(mesh):
    return jax.shard_map(
        on_device,
        mesh=mesh,
        in_specs=(
            P("rep", None, None, "space"),
            P("rep", None, "space"),
            P("rep", None, "space"),
            P("rep", "space"),
            P("rep", None, "space"),
            P("rep", "space"),
            P(),
            P(),
            P(),
        ),
        out_specs=P("rep", None, None, "space"),
        check_vma=False,
    )
```

```python
import jax
import jax.numpy as jnp
from jax import lax
from jax.experimental import pallas as pl
from jax.experimental.pallas import tpu as pltpu
from jax.sharding import PartitionSpec as P

STEPS = 2
LANES = 128

time_step = 0.2
softening = 0.5

VMEM = pl.BlockSpec(memory_space=pltpu.VMEM)
MESH = pl.DeviceIdType.MESH
f32 = jnp.float32
i32 = jnp.int32
bf16 = jnp.bfloat16

WIDE = 256
WIDE_QUADS = 1

POS = 32766.0
UNIT = 1.0 / (POS * 65536)
Q_STEPS = 8191.0
E_STEPS = 32767.0


def upper_half():
    return lax.broadcasted_iota(i32, (8, LANES), 0) >= 4


def row(values):
    return jnp.broadcast_to(values, (8, LANES))


def twice(tile):
    return jnp.concatenate([tile, tile], 0)


def lookup(tabs, first, count, low, high):
    bits = max(count - 1, 0).bit_length()
    masks = [(high & (1 << b)) != 0 for b in range(bits)]

    def find(tab, bit, start):
        if bit < 0:
            return jnp.take_along_axis(tab[first + start], low, axis=1)
        lower = find(tab, bit - 1, start)
        if start + (1 << bit) >= count:
            return lower
        return jnp.where(masks[bit], find(tab, bit - 1, start + (1 << bit)), lower)

    return [find(tab, bits - 1, 0) for tab in tabs]


def quad_index(near, quad, base):
    rows = [row(near[4 * quad + n : 4 * quad + n + 1, pl.ds(base, LANES)]) for n in range(4)]
    sublane = lax.broadcasted_iota(i32, (8, LANES), 0)
    return jnp.where(
        sublane < 4,
        jnp.where(sublane < 2, rows[0], rows[1]),
        jnp.where(sublane < 6, rows[2], rows[3]),
    )


def two_rows(first, second):
    odd = (lax.broadcasted_iota(i32, (8, LANES), 0) & 1) == 1
    return jnp.where(odd, row(second), row(first))


def low16(word):
    return (word << 16) >> 16


def fill_exact(tab, block):
    for k in range(block.shape[1] // LANES):
        tab[k] = twice(block[:, k * LANES : (k + 1) * LANES])


def gather_ghosts(tab, comps, own, gs, out_first, out_last):
    width = out_first.shape[2]
    up = upper_half()
    for g in range(width // LANES):
        index = jnp.where(
            up,
            row(gs[:, width + g * LANES : width + (g + 1) * LANES]),
            row(gs[:, g * LANES : (g + 1) * LANES]),
        )
        found = lookup([tab.at[c] for c in range(comps)], 0, own, index & (LANES - 1), index >> 7)
        for c in range(comps):
            out_first[c, :, g * LANES : (g + 1) * LANES] = found[c][:4]
            out_last[c, :, g * LANES : (g + 1) * LANES] = found[c][4:]


def pack_params(tabs, first, par):
    for k in range(par.shape[2] // LANES):
        cut = slice(k * LANES, (k + 1) * LANES)
        q = (par[0, :, cut] * Q_STEPS + 32768.5).astype(i32) - 32768
        e = (par[1, :, cut] * E_STEPS + 0.5).astype(i32)
        word = (q << 16) | e
        for half in range(2):
            tabs[half][first + k] = two_rows(word[2 * half : 2 * half + 1], word[2 * half + 1 : 2 * half + 2])


def largest(blocks):
    top = None
    for block in blocks:
        for c in range(3):
            here = jnp.max(jnp.abs(block[c]), axis=0, keepdims=True)
            here = jnp.max(here, axis=1, keepdims=True)
            top = here if top is None else jnp.maximum(top, here)
    return jnp.maximum(top, 1e-30)


def both_halves(high, low):
    low = ((low + 32768.5).astype(i32) - 32768) & 65535
    high = (high + 32768.5 - low.astype(f32) * (1.0 / 65536)).astype(i32) - 32768
    return (high << 16) | low


def pack_positions(tabs, first, pos, top):
    factor = POS / top
    for k in range(pos.shape[2] // LANES):
        cut = slice(k * LANES, (k + 1) * LANES)
        x, y, z = [pos[c, :, cut] * factor for c in range(3)]
        word = both_halves(x, y)
        depth = both_halves(z[0:2], z[2:4])
        tabs[0][first + k] = two_rows(word[0:1], word[1:2])
        tabs[1][first + k] = two_rows(word[2:3], word[3:4])
        tabs[2][first + k] = two_rows(depth[0:1], depth[1:2])


def unpack_positions(words, unit):
    third = (words[2], words[2] << 16)
    return [
        [v.astype(f32) * unit for v in (words[half], words[half] << 16, third[half])] for half in range(2)
    ]


def wide_pieces(block, c):
    return [block[c, :, k * WIDE : (k + 1) * WIDE] for k in range(block.shape[2] // WIDE)]


def fill_wide(tab, first, comps, blocks):
    per_comp = tab.shape[1] // comps
    for c in range(comps):
        pieces = [piece for block in blocks for piece in wide_pieces(block, c)]
        for k in range(0, len(pieces), 4):
            stack = jnp.concatenate(pieces[k : k + 4], 0)
            big = stack.astype(bf16)
            rows = pl.ds(c * per_comp + (first + k) * 4, 16)
            tab[0, rows, :] = big
            tab[1, rows, :] = (stack - big.astype(f32)).astype(bf16)


def wide_rows(near, quad, tile, base):
    first = 4 * quad + 2 * tile
    return [near[n : n + 1, pl.ds(base, LANES)] for n in (first, first + 1)]


def one_hot(rows):
    slot = lax.broadcasted_iota(i32, (WIDE, LANES), 0).astype(f32).astype(bf16)
    one, zero = jnp.ones((WIDE, LANES), bf16), jnp.zeros((WIDE, LANES), bf16)
    hits = []
    for r in rows:
        low = jnp.broadcast_to((r & (WIDE - 1)).astype(f32), (WIDE, LANES)).astype(bf16)
        hits.append(jnp.where(slot == low, one, zero))
    return jnp.concatenate(hits, 1)


def wide_find(tab, comps, weights, rows):
    found = jnp.dot(tab[0], weights, preferred_element_type=f32) + jnp.dot(
        tab[1], weights, preferred_element_type=f32
    )
    pairs = tab.shape[1] // comps // 8
    bits = max(pairs - 1, 0).bit_length()
    up = upper_half()
    highs = [row(r) >> 8 for r in rows]
    masks = [[(high & (2 << b)) != 0 for b in range(bits)] for high in highs]
    even = ((jnp.where(up, highs[1], highs[0]) & 1) == 1) == up

    def choose(c, side, bit, start):
        if bit < 0:
            top = (c * pairs + start) * 8
            return found[top : top + 8, side * LANES : (side + 1) * LANES]
        lower = choose(c, side, bit - 1, start)
        if start + (1 << bit) >= pairs:
            return lower
        return jnp.where(masks[side][bit], choose(c, side, bit - 1, start + (1 << bit)), lower)

    out = []
    for c in range(comps):
        a, b = choose(c, 0, bits - 1, 0), choose(c, 1, bits - 1, 0)
        crossed = pltpu.roll(jnp.where(up, a, b), 4, 0)
        out.append(jnp.where(even, jnp.where(up, b, a), crossed))
    return out


def fold(parts):
    sublane = lax.broadcasted_iota(i32, (8, LANES), 0)
    up, second = sublane >= 4, (sublane & 2) != 0
    outer = [
        jnp.where(up, b, a) + pltpu.roll(jnp.where(up, a, b), 4, 0)
        for a, b in ((parts[0], parts[2]), (parts[1], parts[3]))
    ]
    swapped = jnp.take_along_axis(jnp.where(second, outer[0], outer[1]), sublane ^ 2, axis=0)
    inner = jnp.where(second, outer[1], outer[0]) + swapped
    even = (sublane * 2) & 7
    both = jnp.take_along_axis(inner, even, axis=0) + jnp.take_along_axis(inner, even + 1, axis=0)
    return both[:4]


def forces(pos, ratio, lanes, there, params, quads):
    force = [[None] * 4 for _ in range(3)]
    for quad in range(quads):
        for half in range(2):
            other = [there[quad, half, c] for c in range(3)]
            charge, depth = params[quad, half, 0], params[quad, half, 1]
            for i in range(4):
                offset = [row(pos[c, i : i + 1, lanes]) - other[c] for c in range(3)]
                square = offset[0] * offset[0] + (offset[1] * offset[1] + (offset[2] * offset[2] + softening))
                root = lax.rsqrt(square)
                cube = root * root * root
                weight = cube * (row(ratio[i : i + 1, lanes]) * charge + depth * (cube - root))
                for c in range(3):
                    term = weight * offset[c]
                    force[c][i] = term if quad + half == 0 else force[c][i] + term
    return [fold(force[c]) for c in range(3)]


def kernel(
    partner_in, order_in, coupling_in, phase_in, charges_in, lj_in, fill_in, near_in, gs_in, out,
    partner, scale_order, coupling, phase, charges, lj, fill, near, gs, ratio, spot_even, spot_odd,
    from_low, from_high, par, par_first, par_last, par_low, par_high,
    pos_first, pos_last, pos_low, pos_high, pos, pos_next, vel,
    exact, packed_par, packed_pos, gathered, part, part_par, wide_par, wide_pos, hot, ready_sem, load_sem, send_sem, recv_sem,
):
    total, width = phase.shape[2], gs.shape[1] // 2
    own, ghost = total // LANES, width // LANES
    tiles = own + 2 * ghost
    early = own - own // 4
    quads = near.shape[0] // 4
    slim = quads - WIDE_QUADS
    level, levels = lax.axis_index("rep"), lax.axis_size("rep")
    place, places = lax.axis_index("space"), lax.axis_size("space")
    has_low, has_high = level > 0, level < levels - 1
    above, below = lax.rem(place + 1, places), lax.rem(place + places - 1, places)

    barrier = pltpu.get_barrier_semaphore()

    def greet(device):
        pl.semaphore_signal(barrier, inc=1, device_id=device, device_id_type=MESH)

    odd = lax.rem(place, 2) == 1

    @pl.when(jnp.logical_not(odd))
    def _():
        greet({"space": above})
        greet({"space": below})

    @pl.when(has_low)
    def _():
        greet({"rep": level - 1})

    @pl.when(has_high)
    def _():
        greet({"rep": level + 1})

    loads = [
        pltpu.make_async_copy(src, dst, load_sem.at[n])
        for n, (src, dst) in enumerate(
            [
                (phase_in, phase), (fill_in, fill), (charges_in, charges), (lj_in, lj), (gs_in, gs), (near_in, near),
                (partner_in, partner), (order_in, scale_order), (coupling_in, coupling),
            ]
        )
    ]
    for copy in loads:
        copy.start()

    def remote(src, dst, number, device):
        return pltpu.make_async_remote_copy(
            src_ref=src, dst_ref=dst, send_sem=send_sem.at[number], recv_sem=recv_sem.at[number],
            device_id=device, device_id_type=MESH,
        )

    def ring(first, last, low, high, number):
        return [remote(last, low, number, {"space": above}), remote(first, high, number + 1, {"space": below})]

    def each_group(start, stop, body, unroll=4):
        def step(group, carry):
            body(group, pl.multiple_of(group * LANES, LANES))
            return carry

        lax.fori_loop(start, stop, step, 0, unroll=unroll)

    pl.semaphore_wait(barrier, jnp.where(odd, 2, 0) + jnp.where(has_low, 1, 0) + jnp.where(has_high, 1, 0))

    @pl.when(odd)
    def _():
        for neighbour in (above, below):
            pl.semaphore_signal(ready_sem, inc=1, device_id={"space": neighbour}, device_id_type=MESH)

    halves = (pl.ds(0, 3), pl.ds(3, 3))
    rising = [remote(phase_in.at[h], from_low.at[h], n, {"rep": level + 1}) for n, h in enumerate(halves)]
    falling = [remote(phase_in.at[h], from_high.at[h], 2 + n, {"rep": level - 1}) for n, h in enumerate(halves)]

    def swap_start(n):
        @pl.when(has_high)
        def _():
            rising[n].start()

        @pl.when(has_low)
        def _():
            falling[n].start()

    def swap_arrived(n):
        @pl.when(has_low)
        def _():
            rising[n].wait_recv()

        @pl.when(has_high)
        def _():
            falling[n].wait_recv()

    swap_start(0)

    for copy in loads[1:5]:
        copy.wait()
    slot = lax.broadcasted_iota(i32, (4, total), 0)
    present = (slot < fill[...]).astype(f32)
    par[0] = charges[...] * present
    par[1] = lj[...] * present
    ratio[...] = charges[...] / lj[...]
    for c in range(2):
        fill_exact(exact.at[c], par[c])
    gather_ghosts(exact, 2, own, gs, par_first, par_last)
    par_tabs = [packed_par.at[0], packed_par.at[1]]
    pack_params(par_tabs, 0, par)
    fill_wide(wide_par, 0, 2, [par])

    def look_ahead(tabs, kept, group, base):
        for quad in range(slim):
            index = quad_index(near, quad, base)
            for n, word in enumerate(lookup(tabs, 0, own, index & (LANES - 1), index >> 7)):
                kept[group, quad, n] = word

    def params_ahead(group, base):
        look_ahead(par_tabs, part_par, group, base)
        for quad in range(slim, quads):
            for tile in range(2):
                hot[group, quad - slim, tile] = one_hot(wide_rows(near, quad, tile, base))

    for copy in loads[:1] + loads[5:]:
        copy.wait()
    each_group(0, early, params_ahead)


    def find_rest(tabs, kept, group, quad, index):
        words = lookup(tabs, own, tiles - own, index & (LANES - 1), (index >> 7) - own)
        return [jnp.where(index < total, kept[group, quad, n], word) for n, word in enumerate(words)]

    moved = partner[level] - level

    def swapped(c, lanes):
        return jnp.where(
            moved == 0, phase[c, :, lanes],
            jnp.where(moved < 0, from_low[c, :, lanes], from_high[c, :, lanes]),
        )

    swap_arrived(0)
    for c in range(3):
        block = swapped(c, pl.ds(0, total))
        pos[c] = block
        fill_exact(exact.at[c], block)
    gather_ghosts(exact, 3, own, gs, pos_first.at[0], pos_last.at[0])
    pos_rings = [
        ring(pos_first.at[n], pos_last.at[n], pos_low.at[n], pos_high.at[n], 6 + 2 * n) for n in range(2)
    ]
    par_ring = ring(par_first, par_last, par_low, par_high, 4)

    @pl.when(jnp.logical_not(odd))
    def _():
        pl.semaphore_wait(ready_sem, 2)

    for copy in par_ring + pos_rings[0]:
        copy.start()
    swap_start(1)
    tabs = [packed_pos.at[n] for n in range(3)]
    top_own = largest([pos])
    pack_positions(tabs, 0, pos, top_own)
    fill_wide(wide_pos, 0, 3, [pos])
    unit_own = top_own * UNIT

    each_group(0, own, lambda group, base: look_ahead(tabs, part, group, base), 8)
    each_group(early, own, params_ahead)

    for copy in par_ring:
        copy.wait_recv()
    pack_params(par_tabs, own, par_low)
    pack_params(par_tabs, own + ghost, par_high)
    wide_own = total // WIDE
    fill_wide(wide_par, wide_own, 2, [par_low, par_high])
    strength = coupling[scale_order[level]]

    def wide_params(group, base):
        for quad in range(slim, quads):
            for tile in range(2):
                rows = wide_rows(near, quad, tile, base)
                charge, depth = wide_find(wide_par, 2, hot[group, quad - slim, tile], rows)
                gathered[group, quad, tile, 0] = charge * strength
                gathered[group, quad, tile, 1] = depth

    def finish_params(group):
        base = pl.multiple_of(group * LANES, LANES)
        for quad in range(slim):
            words = find_rest(par_tabs, part_par, group, quad, quad_index(near, quad, base))
            for half, word in enumerate(words):
                gathered[group, quad, half, 0] = (word >> 16).astype(f32) * (strength * (1.0 / Q_STEPS))
                gathered[group, quad, half, 1] = (word & 65535).astype(f32) * (1.0 / E_STEPS)

    def ghosts_arrived(n):
        for copy in pos_rings[n]:
            copy.wait_recv()
        low, high = pos_low.at[n], pos_high.at[n]
        top = largest([low, high])
        pack_positions(tabs, own, low, top)
        pack_positions(tabs, own + ghost, high, top)
        fill_wide(wide_pos, wide_own, 3, [low, high])
        return top * UNIT

    def find(group, spot, unit_here, unit_there):
        base = pl.multiple_of(group * LANES, LANES)
        for quad in range(quads):
            if quad < slim:
                index = quad_index(near, quad, base)
                words = find_rest(tabs, part, group, quad, index)
                pair = unpack_positions(words, jnp.where(index < total, unit_here, unit_there))
            else:
                pair = [
                    wide_find(wide_pos, 3, hot[group, quad - slim, tile], wide_rows(near, quad, tile, base))
                    for tile in range(2)
                ]
            for half in range(2):
                for c in range(3):
                    spot[quad, half, c] = pair[half][c]

    def move_all(move, prepare):
        prepare(0, spot_even)
        for group in range(own):
            here, there = (spot_even, spot_odd) if group % 2 == 0 else (spot_odd, spot_even)
            move(group, here)
            if group + 1 < own:
                prepare(group + 1, there)

    def force_on(where, group, spot):
        lanes = pl.ds(pl.multiple_of(group * LANES, LANES), LANES)
        depth = par[1, :, lanes]
        return lanes, [f * depth for f in forces(where, ratio, lanes, spot, gathered.at[group], quads)]

    swap_arrived(1)
    unit_ghost = ghosts_arrived(0)

    def first_step(group, spot):
        lanes, force = force_on(pos, group, spot)
        for c in range(3):
            v = swapped(3 + c, lanes) + time_step * force[c]
            vel[c, :, lanes] = v
            pos_next[c, :, lanes] = pos[c, :, lanes] + time_step * v

    def first_prepare(group, spot):
        finish_params(group)
        wide_params(group, pl.multiple_of(group * LANES, LANES))
        find(group, spot, unit_own, unit_ghost)

    move_all(first_step, first_prepare)

    for c in range(3):
        fill_exact(exact.at[c], pos_next[c])
    gather_ghosts(exact, 3, own, gs, pos_first.at[1], pos_last.at[1])
    for copy in pos_rings[1]:
        copy.start()
    top_own = largest([pos_next])
    pack_positions(tabs, 0, pos_next, top_own)
    fill_wide(wide_pos, 0, 3, [pos_next])
    unit_own_next = top_own * UNIT

    each_group(0, own, lambda group, base: look_ahead(tabs, part, group, base), 8)
    unit_ghost_next = ghosts_arrived(1)

    def second_step(group, spot):
        lanes, force = force_on(pos_next, group, spot)
        for c in range(3):
            v = vel[c, :, lanes] + time_step * force[c]
            out[3 + c, :, lanes] = v
            out[c, :, lanes] = pos_next[c, :, lanes] + time_step * v

    move_all(second_step, lambda group, spot: find(group, spot, unit_own_next, unit_ghost_next))

    for copy in par_ring + pos_rings[0] + pos_rings[1]:
        copy.wait_send()
    for n in range(2):

        @pl.when(has_high)
        def _():
            rising[n].wait_send()

        @pl.when(has_low)
        def _():
            falling[n].wait_send()


def on_device(
    phase_space, charges, lj_depth, cluster_fill, neighbours, ghost_send, partner, scale_order, coupling
):
    phase = phase_space[0]
    rows, slots, total = phase.shape
    width = ghost_send.shape[1] // 2
    own = total // LANES
    tiles = own + 2 * (width // LANES)
    quads = neighbours.shape[1] // 4
    wides = tiles * LANES // WIDE
    out = pl.pallas_call(
        kernel,
        out_shape=pltpu.VMEM(phase.shape, f32),
        in_specs=[pl.BlockSpec(memory_space=pltpu.HBM)] * 9,
        out_specs=VMEM,
        scratch_shapes=[
            pltpu.SMEM(partner.shape, i32),
            pltpu.SMEM(scale_order.shape, i32),
            pltpu.SMEM(coupling.shape, f32),
            pltpu.VMEM((rows, slots, total), f32),
            pltpu.VMEM((slots, total), f32),
            pltpu.VMEM((slots, total), f32),
            pltpu.VMEM((1, total), i32),
            pltpu.VMEM((4 * quads, total), i32),
            pltpu.VMEM((1, 2 * width), i32),
            pltpu.VMEM((slots, total), f32),
            pltpu.VMEM((quads, 2, 3, 8, LANES), f32),
            pltpu.VMEM((quads, 2, 3, 8, LANES), f32),
            pltpu.VMEM((rows, slots, total), f32),
            pltpu.VMEM((rows, slots, total), f32),
            pltpu.VMEM((2, slots, total), f32),
        ]
        + [pltpu.VMEM((2, slots, width), f32)] * 4
        + [pltpu.VMEM((2, 3, slots, width), f32)] * 4
        + [pltpu.VMEM((3, slots, total), f32)] * 3
        + [
            pltpu.VMEM((3, own, 8, LANES), f32),
            pltpu.VMEM((2, tiles, 8, LANES), i32),
            pltpu.VMEM((3, tiles, 8, LANES), i32),
            pltpu.VMEM((own, quads, 2, 2, 8, LANES), f32),
            pltpu.VMEM((own, quads - WIDE_QUADS, 3, 8, LANES), i32),
            pltpu.VMEM((own, quads - WIDE_QUADS, 2, 8, LANES), i32),
            pltpu.VMEM((2, 2 * 4 * wides, WIDE), bf16),
            pltpu.VMEM((2, 3 * 4 * wides, WIDE), bf16),
            pltpu.VMEM((own, WIDE_QUADS, 2, WIDE, 2 * LANES), bf16),
            pltpu.SemaphoreType.REGULAR,
            pltpu.SemaphoreType.DMA((9,)),
            pltpu.SemaphoreType.DMA((10,)),
            pltpu.SemaphoreType.DMA((10,)),
        ],
        compiler_params=pltpu.CompilerParams(collective_id=0, has_side_effects=True),
    )(partner, scale_order, coupling, phase, charges[0], lj_depth[0], cluster_fill, neighbours[0], ghost_send)
    return out[None]


def solution(mesh):
    return jax.shard_map(
        on_device,
        mesh=mesh,
        in_specs=(
            P("rep", None, None, "space"),
            P("rep", None, "space"),
            P("rep", None, "space"),
            P("rep", "space"),
            P("rep", None, "space"),
            P("rep", "space"),
            P(),
            P(),
            P(),
        ),
        out_specs=P("rep", None, None, "space"),
        check_vma=False,
    )
```
